32 devices in a mesh: chan: 8 (over y, x, core), filt: 4 (over z).
Axes of the slice: x: 2, y: 2, z: 4, core: 2. Of those that a mesh axis runs over, the one named last changes fastest.
Arguments:
- activations: bfloat16 [2592, 2048], P(None, ('chan', 'filt')), may hold values from -6 to 6
- act_tangent: bfloat16 [2592, 2048], P(None, ('chan', 'filt')), may hold values from -6 to 6
- kernel: bfloat16 [9, 2048, 2048], P(None, 'chan', 'filt'), may hold values from -0.046875 to 0.046875
- kernel_tangent: bfloat16 [9, 2048, 2048], P(None, 'chan', 'filt'), may hold values from -0.046875 to 0.046875
- slope: bfloat16 [2592, 2048], P('chan', 'filt'), may hold values from 0.19921875 to 1.09375
- curvature: bfloat16 [2592, 2048], P('chan', 'filt'), may hold values from 0.29882812 to 3
Outputs:
- input_cotangent: bfloat16 [2592, 2048], P('filt', 'chan')
- kernel_product: float32 [9, 2048, 2048], P(None, 'chan', 'filt')
The draws below stay inside these ranges and needn't reach their ends.
All inputs are finite; a program needn't handle non-finite values.
Results may differ from the reference program's by a relative error of at most 0.0047.
Values may be sent and summed in bfloat16 or wider, within the bound.
No kernel may reach another device: no remote copies, remote signals or barrier semaphores. Data moves between devices by JAX's collectives and lax.ppermute only.
A program may use at most 192 MiB of HBM per device.

```python
import math
import jax
import jax.numpy as jnp

C = 2048
F = 2048
HH = 12
WW = 12
PIXELS = 2592


def level_of(key, extent, pieces, least, largest):
    level = 1.0
    for position, shards_of in pieces:
        heights = jax.random.uniform(jax.random.fold_in(jax.random.fold_in(key, 6), position), (shards_of,), jnp.float32, least / len(pieces), largest / len(pieces))
        level = level * jnp.repeat(jnp.exp(heights), extent[position] // shards_of).reshape((-1,) + (1,) * (len(extent) - 1 - position))
    return level


def scatter_about(key, shape, scale, reach, cuts=(), dtype=jnp.bfloat16):
    values = scale * jax.random.normal(key, shape, jnp.float32)
    if cuts:
        values = values * level_of(key, shape, cuts, -0.22, 0.18)
    return jnp.clip(values, -reach, reach).astype(dtype)


def setup_inputs(seed: int = 0) -> dict:
    seeds = jax.random.split(jax.random.key(seed), 7)
    activations = scatter_about(seeds[0], (PIXELS, C), 1.0, 6.0, ((1, 32),))
    act_tangent = scatter_about(seeds[1], (PIXELS, C), 1.0, 6.0, ((1, 32),))
    kernel = scatter_about(seeds[2], (9, C, F), (9 * C) ** -0.5, 0.046875, ((1, 8), (2, 4)))
    kernel_tangent = scatter_about(seeds[3], (9, C, F), (9 * C) ** -0.5, 0.046875, ((1, 8), (2, 4)))
    slope = jnp.clip(0.19921875 + 0.89453125 * jax.random.uniform(seeds[4], (PIXELS, F), jnp.float32) ** level_of(seeds[4], (PIXELS, F), ((0, 8), (1, 4)), -0.2, 0.2), 0.19921875, 1.09375).astype(jnp.bfloat16)
    curvature = jnp.clip(jnp.exp(math.log(3.0) - 2.306499 * jax.random.uniform(seeds[5], (PIXELS, F), jnp.float32) ** level_of(seeds[5], (PIXELS, F), ((0, 8), (1, 4)), -0.2, 0.2)), 0.29882812, 3.0).astype(jnp.bfloat16)
    return {"activations": activations, "act_tangent": act_tangent, "kernel": kernel, "kernel_tangent": kernel_tangent, "slope": slope, "curvature": curvature}


def windows(flat, flip):
    width = flat.shape[-1]
    image = flat.reshape(-1, HH, WW, width)
    padded = jnp.pad(image, ((0, 0), (1, 1), (1, 1), (0, 0)))
    result = []
    for row_tap in range(3):
        for col_tap in range(3):
            top = 2 - row_tap if flip else row_tap
            left = 2 - col_tap if flip else col_tap
            result.append(padded[:, top:top + HH, left:left + WW, :].reshape(-1, width))
    return result

def reference(activations, act_tangent, kernel, kernel_tangent, slope, curvature):
    acts = windows(activations, False)
    tans = windows(act_tangent, False)
    out_tangent = jnp.zeros((PIXELS, F), jnp.float32)
    for tap in range(9):
        out_tangent = out_tangent + jnp.dot(tans[tap], kernel[tap], preferred_element_type=jnp.float32)
        out_tangent = out_tangent + jnp.dot(acts[tap], kernel_tangent[tap], preferred_element_type=jnp.float32)
    slope_f = slope.astype(jnp.float32)
    weighted = (slope_f * slope_f * curvature.astype(jnp.float32) * out_tangent).astype(jnp.bfloat16)
    backs = windows(weighted, True)
    cotangent = jnp.zeros((PIXELS, C), jnp.float32)
    grads = []
    for tap in range(9):
        cotangent = cotangent + jnp.dot(backs[tap], kernel[tap].T, preferred_element_type=jnp.float32)
        grads.append(jnp.dot(acts[tap].T, weighted, preferred_element_type=jnp.float32))
    kernel_product = jnp.stack(grads) / jnp.sqrt(jnp.float32(PIXELS))
    return (cotangent.astype(jnp.bfloat16), kernel_product)
```

```python
import functools

import jax
import jax.numpy as jnp
from jax import lax
from jax.experimental import pallas as pl
from jax.experimental.pallas import tpu as pltpu
from jax.sharding import PartitionSpec as P

HH = 12
WW = 12
LANES = 128
STRIPS = 4
DEEP = HH // STRIPS
PAIR = 2
EIGHT = PAIR * STRIPS
PIECE = WW * EIGHT
GROUP = DEEP * PIECE


def windows(flat, flip):
    width = flat.shape[-1]
    image = flat.reshape(-1, HH, WW, width)
    padded = jnp.pad(image, ((0, 0), (1, 1), (1, 1), (0, 0)))
    result = []
    for row_tap in range(3):
        for col_tap in range(3):
            top = 2 - row_tap if flip else row_tap
            left = 2 - col_tap if flip else col_tap
            result.append(padded[:, top : top + HH, left : left + WW, :].reshape(-1, width))
    return result


def weigh(slope, curvature, tangent):
    slope_f = slope.astype(jnp.float32)
    return (slope_f * slope_f * curvature.astype(jnp.float32) * tangent).astype(jnp.bfloat16)


def any_device(activations, act_tangent, kernel, kernel_tangent, slope, curvature):
    acts_block, tans_block = (
        lax.all_gather(activations, "filt", axis=1, tiled=True),
        lax.all_gather(act_tangent, "filt", axis=1, tiled=True),
    )
    acts = windows(acts_block, False)
    tans = windows(tans_block, False)
    pixel_count = acts_block.shape[0]
    partial_value = jnp.zeros((pixel_count, kernel.shape[2]), jnp.float32)
    for tap in range(9):
        partial_value = partial_value + jnp.dot(
            tans[tap], kernel[tap], preferred_element_type=jnp.float32
        )
        partial_value = partial_value + jnp.dot(
            acts[tap], kernel_tangent[tap], preferred_element_type=jnp.float32
        )
    total = lax.psum(partial_value, "chan")
    slope_all, curve_all = (
        lax.all_gather(slope, "chan", axis=0, tiled=True),
        lax.all_gather(curvature, "chan", axis=0, tiled=True),
    )
    weighted = weigh(slope_all, curve_all, total)
    backs = windows(weighted, True)
    cot_part = jnp.zeros((pixel_count, kernel.shape[1]), jnp.float32)
    grads = []
    for tap in range(9):
        cot_part = cot_part + lax.dot_general(
            backs[tap], kernel[tap], (((1,), (1,)), ((), ())), preferred_element_type=jnp.float32
        )
        grads.append(
            lax.dot_general(
                acts[tap], weighted, (((0,), (0,)), ((), ())), preferred_element_type=jnp.float32
            )
        )
    kernel_product = jnp.stack(grads) / jnp.sqrt(jnp.float32(pixel_count))
    cotangent = lax.psum_scatter(cot_part, "filt", scatter_dimension=0, tiled=True).astype(
        jnp.bfloat16
    )
    return (cotangent, kernel_product)


def pieces_of(groups):
    for g, images in enumerate(groups):
        for strip in range(EIGHT):
            image, part = images[strip // STRIPS], strip % STRIPS
            for deep in range(DEEP):
                source = (image * HH + part * DEEP + deep) * WW
                yield g, strip, deep, source, (deep * len(groups) + g) * PIECE + strip


def sort_kernel(chunks, x_ref, *refs):
    outs, (flat, sorted_) = refs[: len(chunks)], refs[len(chunks) :]
    for lane in range(0, x_ref.shape[1], LANES):
        cols = pl.ds(lane, LANES)
        flat[...] = x_ref[:, cols].astype(jnp.float32)
        for groups, out in zip(chunks, outs):
            for _, _, _, source, target in pieces_of(groups):
                sorted_[pl.ds(target, WW, stride=EIGHT), :] = flat[pl.ds(source, WW), :]
            out[:, cols] = sorted_[pl.ds(0, out.shape[0]), :].astype(out.dtype)


def sort_rows(x, chunks):
    rows = [len(groups) * GROUP for groups in chunks]
    return pl.pallas_call(
        functools.partial(sort_kernel, chunks),
        out_shape=[jax.ShapeDtypeStruct((r, x.shape[1]), x.dtype) for r in rows],
        scratch_shapes=[
            pltpu.VMEM((x.shape[0], LANES), jnp.float32),
            pltpu.VMEM((max(rows), LANES), jnp.float32),
        ],
        name="sort_rows",
    )(x)


def build(x_ref, views, groups):
    width = x_ref.shape[1]
    strip = lax.broadcasted_iota(jnp.int32, (PIECE, width), 0) % STRIPS

    def put(at, block):
        at = pl.multiple_of(at, PIECE)
        none = jnp.zeros((EIGHT, width), jnp.float32)
        views[1, pl.ds(at, PIECE), :] = block.astype(jnp.bfloat16)
        before = jnp.concatenate([none, block[: PIECE - EIGHT]], axis=0)
        views[0, pl.ds(at, PIECE), :] = before.astype(jnp.bfloat16)
        after = jnp.concatenate([block[EIGHT:], none], axis=0)
        views[2, pl.ds(at, PIECE), :] = after.astype(jnp.bfloat16)

    def load(at):
        return x_ref[pl.ds(pl.multiple_of(at, PIECE), PIECE), :].astype(jnp.float32)

    def turn(block, by):
        return pltpu.roll(block.reshape(WW, EIGHT, width), by, 1).reshape(PIECE, width)

    @pl.loop(0, DEEP * groups)
    def _(n):
        put((groups + n) * PIECE, load(n * PIECE))

    @pl.loop(0, groups)
    def _(g):
        above = turn(load(((DEEP - 1) * groups + g) * PIECE), 1)
        put(g * PIECE, jnp.where(strip == 0, 0.0, above))
        below = turn(load(g * PIECE), EIGHT - 1)
        put(((DEEP + 1) * groups + g) * PIECE, jnp.where(strip == STRIPS - 1, 0.0, below))


def tap_rows(views, groups, tap, flip):
    row, col = tap // 3, lax.rem(tap, 3)
    if flip:
        row, col = 2 - row, 2 - col
    start = pl.multiple_of(row * (groups * PIECE), PIECE)
    return views[col, pl.ds(start, groups * GROUP), :]


def views_shape(groups, width):
    return pltpu.VMEM((3, (DEEP + 2) * groups * PIECE, width), jnp.bfloat16)


def tangent_kernel(groups, half_ref, x_ref, w_ref, send_ref, keep_ref, views, acc):
    tap = pl.program_id(0)

    @pl.when(tap == 0)
    def _():
        build(x_ref, views, groups)
        acc[...] = jnp.zeros_like(acc)

    acc[...] += jnp.dot(
        tap_rows(views, groups, tap, False), w_ref[0], preferred_element_type=jnp.float32
    )

    @pl.when(tap == 8)
    def _():
        half = half_ref[0]
        rows = keep_ref.shape[0]
        mine = pl.ds(pl.multiple_of(half * rows, rows), rows)
        other = pl.ds(pl.multiple_of((1 - half) * rows, rows), rows)
        send_ref[...] = acc[other, :].astype(jnp.bfloat16)
        keep_ref[...] = acc[mine, :]


def tangent(half, x, w, groups):
    rows, width = x.shape
    filters = w.shape[2]
    return pl.pallas_call(
        functools.partial(tangent_kernel, groups),
        grid_spec=pltpu.PrefetchScalarGridSpec(
            num_scalar_prefetch=1,
            grid=(9,),
            in_specs=[
                pl.BlockSpec((rows, width), lambda t, h: (0, 0)),
                pl.BlockSpec((1, width, filters), lambda t, h: (t, 0, 0)),
            ],
            out_specs=[pl.BlockSpec((rows // 2, filters), lambda t, h: (0, 0))] * 2,
            scratch_shapes=[views_shape(groups, width), pltpu.VMEM((rows, filters), jnp.float32)],
        ),
        out_shape=[
            jax.ShapeDtypeStruct((rows // 2, filters), jnp.bfloat16),
            jax.ShapeDtypeStruct((rows // 2, filters), jnp.float32),
        ],
        cost_estimate=pl.CostEstimate(
            flops=18 * rows * width * filters, bytes_accessed=2 * w.size, transcendentals=0
        ),
        name="tangent",
    )(half, x, w)


def cotangent_kernel(groups, places, x_ref, w_ref, out_ref, views, acc, flat):
    tap = pl.program_id(0)

    @pl.when(tap == 0)
    def _():
        build(x_ref, views, len(groups))
        acc[...] = jnp.zeros_like(acc)

    lhs = tap_rows(views, len(groups), tap, True)
    for n in range(acc.shape[0]):
        acc[n] += lax.dot_general(
            lhs,
            w_ref[0, n * LANES : (n + 1) * LANES, :],
            (((1,), (1,)), ((), ())),
            preferred_element_type=jnp.float32,
        )

    @pl.when(tap == 8)
    def _():
        for n in range(acc.shape[0]):
            for g, strip, deep, _, row in pieces_of(groups):
                target = places(g, strip) + deep * WW
                flat[pl.ds(target, WW), :] = acc[n, pl.ds(row, WW, stride=EIGHT), :]
            out_ref[:, n * LANES : (n + 1) * LANES] = flat[...].astype(jnp.bfloat16)


def cotangent_part(x, w, groups, places):
    rows, width = x.shape
    channels = w.shape[1]
    return pl.pallas_call(
        functools.partial(cotangent_kernel, groups, places),
        grid=(9,),
        in_specs=[
            pl.BlockSpec((rows, width), lambda t: (0, 0)),
            pl.BlockSpec((1, channels, width), lambda t: (t, 0, 0)),
        ],
        out_specs=pl.BlockSpec((rows, channels), lambda t: (0, 0)),
        scratch_shapes=[
            views_shape(len(groups), width),
            pltpu.VMEM((channels // LANES, rows, LANES), jnp.float32),
            pltpu.VMEM((rows, LANES), jnp.float32),
        ],
        out_shape=jax.ShapeDtypeStruct((rows, channels), jnp.bfloat16),
        cost_estimate=pl.CostEstimate(
            flops=18 * rows * width * channels, bytes_accessed=2 * w.size, transcendentals=0
        ),
        name="cotangent",
    )(x, w)


def grad_kernel(groups, scale, with_sum, *refs):
    xt_ref, w_ref = refs[:2]
    out_ref, views = refs[-2:]
    tap = pl.program_id(0)

    @pl.when(tap == 0)
    def _():
        build(w_ref, views, groups)

    value = jnp.dot(
        xt_ref[...], tap_rows(views, groups, tap, True), preferred_element_type=jnp.float32
    )
    if with_sum:
        value = (value + refs[2][0]) * scale
    out_ref[0] = value


def grad(xt, w, groups, so_far=None, scale=None):
    channels, rows = xt.shape
    filters = w.shape[1]
    given = [xt, w] + ([] if so_far is None else [so_far])
    block = pl.BlockSpec((1, channels, filters), lambda t: (t, 0, 0))
    return pl.pallas_call(
        functools.partial(grad_kernel, groups, scale, so_far is not None),
        grid=(9,),
        in_specs=[
            pl.BlockSpec((channels, rows), lambda t: (0, 0)),
            pl.BlockSpec((rows, filters), lambda t: (0, 0)),
        ]
        + [block] * (len(given) - 2),
        out_specs=block,
        scratch_shapes=[views_shape(groups, filters)],
        out_shape=jax.ShapeDtypeStruct((9, channels, filters), jnp.float32),
        cost_estimate=pl.CostEstimate(
            flops=18 * rows * channels * filters,
            bytes_accessed=36 * channels * filters,
            transcendentals=0,
        ),
        name="grad",
    )(*given)


def pick(index, values):
    result = values[-1]
    for i in range(len(values) - 2, -1, -1):
        result = jnp.where(index == i, values[i], result)
    return result


def block_device(activations, act_tangent, kernel, kernel_tangent, slope, curvature):
    z, me = lax.axis_index("filt"), lax.axis_index("chan")
    depth, across = lax.axis_size("filt"), lax.axis_size("chan")
    half, chip = lax.rem(me, 2), me // 2
    chips = across // 2
    pixels, own = activations.shape
    channels, filters = kernel.shape[1:]

    first, second = [], []
    per = 2 * (pixels // (HH * WW)) // depth
    middle = []
    for a in range(0, depth, 2):
        at = a // 2 * per
        second += [(at, at + 1), (at + per - 2, at + per - 1)]
        first += [(at + 2, at + 3), (at + per - 4, at + per - 3)]
        middle.append(at + 4)
    first.append(tuple(middle))
    chunks = [first, second]

    both = jnp.stack([slope, curvature]).reshape(2, -1, chips, LANES)
    both = jnp.repeat(both.transpose(2, 0, 1, 3), 2, axis=0)
    both = lax.all_to_all(both, "chan", 0, 0, tiled=True)
    both = both.transpose(0, 2, 1, 3).reshape(pixels, 2 * LANES)

    mixed = sort_rows(jnp.concatenate([activations, act_tangent], axis=1), chunks)
    factors = sort_rows(both, chunks)

    weights = jnp.stack(
        [kernel_tangent.reshape(9, depth, own, filters), kernel.reshape(9, depth, own, filters)],
        axis=2,
    ).reshape(9, 2 * channels, filters)

    def gathered(x):
        up, down = x, x
        ups, downs = {0: x}, {}
        for step in range(1, depth):
            up = lax.ppermute(up, "filt", [(i, i + 1) for i in range(step - 1, depth - 1)])
            down = lax.ppermute(down, "filt", [(i + 1, i) for i in range(0, depth - step)])
            ups[step], downs[step] = up, down
        shards = []
        for j in range(depth):
            shards.append(pick(z, [ups[i - j] if i >= j else downs[j - i] for i in range(depth)]))
        return jnp.concatenate(shards, axis=1)

    def swap(x, bit):
        return lax.ppermute(x, "chan", [(i, i ^ bit) for i in range(across)])

    def lanes(x, block):
        return lax.dynamic_slice_in_dim(x, block * LANES, LANES, axis=1)

    def weighted(x, factor, groups):
        send, keep = tangent(half.reshape(1), x, weights, groups)
        total = keep + swap(send, 1).astype(jnp.float32)
        mine = lanes(total, chip)
        for m in range(1, chips):
            got = swap(lanes(total, chip ^ m).astype(jnp.bfloat16), 2 * m)
            mine = mine + got.astype(jnp.float32)
        rows = mine.shape[0]
        factor = lax.dynamic_slice_in_dim(factor, half * rows, rows, axis=0)
        w = weigh(factor[:, :LANES], factor[:, LANES:], mine)
        parts = [w] + [swap(w, 2 * m) for m in range(1, chips)]
        w = jnp.concatenate(
            [pick(chip, [parts[b ^ i] for i in range(chips)]) for b in range(chips)], axis=1
        )
        other = swap(w, 1)
        low, high = jnp.where(half == 0, w, other), jnp.where(half == 0, other, w)
        return jnp.concatenate([low, high], axis=0)

    def acts_of(x):
        width = 2 * own
        return jnp.concatenate(
            [x[:, j * width : j * width + own] for j in range(depth)], axis=1
        ).T

    strip_rows = GROUP // EIGHT

    def place_first(g, strip):
        share = first_rows // depth
        if g < depth:
            return g * share + strip * strip_rows
        z_of, rest = divmod(strip, EIGHT // depth)
        return z_of * share + GROUP + rest * strip_rows

    def place_second(g, strip):
        return g * GROUP + strip * strip_rows

    first_rows = len(first) * GROUP

    def spread(part):
        part = lax.all_to_all(
            part.reshape(depth, -1, channels), "filt", 0, 0, tiled=True
        ).astype(jnp.float32)
        total = part[0]
        for j in range(1, depth):
            total = total + part[j]
        return total.astype(jnp.bfloat16)

    x0 = gathered(mixed[0])
    x1 = gathered(mixed[1])
    w0 = weighted(x0, factors[0], len(first))
    c0 = spread(cotangent_part(w0, kernel, first, place_first))
    g0 = grad(acts_of(x0), w0, len(first))
    w1 = weighted(x1, factors[1], len(second))
    c1 = spread(cotangent_part(w1, kernel, second, place_second))
    scale = float(1.0 / (float(pixels) ** 0.5))
    product = grad(acts_of(x1), w1, len(second), g0, scale)

    main, edge = c0[:GROUP], c0[GROUP:]
    result = jnp.where(
        lax.rem(z, 2) == 0,
        jnp.concatenate([c1, main, edge], axis=0),
        jnp.concatenate([edge, main, c1], axis=0),
    )
    return (result, product)


def fits(mesh, pixels, channels, filters):
    depth, across = mesh.shape["filt"], mesh.shape["chan"]
    images = pixels // (HH * WW)
    return (
        depth == 2 * PAIR
        and 2 * images == 9 * depth
        and across == 8
        and 2 * channels == LANES * across * depth
        and filters == LANES * (across // 2) * depth
    )


def solution(mesh):
    in_specs = (
        P(None, ("chan", "filt")),
        P(None, ("chan", "filt")),
        P(None, "chan", "filt"),
        P(None, "chan", "filt"),
        P("chan", "filt"),
        P("chan", "filt"),
    )

    def program(*args):
        pixels, channels = args[0].shape
        body = block_device if fits(mesh, pixels, channels, args[2].shape[2]) else any_device
        return jax.shard_map(
            body,
            mesh=mesh,
            in_specs=in_specs,
            out_specs=(P("filt", "chan"), P(None, "chan", "filt")),
            check_vma=False,
        )(*args)

    return program
```

```python
import functools

import jax
import jax.numpy as jnp
from jax import lax
from jax.experimental import pallas as pl
from jax.experimental.pallas import tpu as pltpu
from jax.sharding import PartitionSpec as P


HH = 12
WW = 12
LANES = 128
STRIPS = 4
DEEP = HH // STRIPS
PAIR = 2
EIGHT = PAIR * STRIPS
PIECE = WW * EIGHT
GROUP = DEEP * PIECE

PARAMS = pltpu.CompilerParams(vmem_limit_bytes=28 << 20)


def windows(flat, flip):
    width = flat.shape[-1]
    image = flat.reshape(-1, HH, WW, width)
    padded = jnp.pad(image, ((0, 0), (1, 1), (1, 1), (0, 0)))
    result = []
    for row_tap in range(3):
        for col_tap in range(3):
            top = 2 - row_tap if flip else row_tap
            left = 2 - col_tap if flip else col_tap
            result.append(padded[:, top : top + HH, left : left + WW, :].reshape(-1, width))
    return result


def weigh(slope, curvature, tangent):
    slope_f = slope.astype(jnp.float32)
    return (slope_f * slope_f * curvature.astype(jnp.float32) * tangent).astype(jnp.bfloat16)


def any_device(activations, act_tangent, kernel, kernel_tangent, slope, curvature):
    acts_block, tans_block = (
        lax.all_gather(activations, "filt", axis=1, tiled=True),
        lax.all_gather(act_tangent, "filt", axis=1, tiled=True),
    )
    acts = windows(acts_block, False)
    tans = windows(tans_block, False)
    pixel_count = acts_block.shape[0]
    partial_value = jnp.zeros((pixel_count, kernel.shape[2]), jnp.float32)
    for tap in range(9):
        partial_value = partial_value + jnp.dot(
            tans[tap], kernel[tap], preferred_element_type=jnp.float32
        )
        partial_value = partial_value + jnp.dot(
            acts[tap], kernel_tangent[tap], preferred_element_type=jnp.float32
        )
    total = lax.psum(partial_value, "chan")
    slope_all, curve_all = (
        lax.all_gather(slope, "chan", axis=0, tiled=True),
        lax.all_gather(curvature, "chan", axis=0, tiled=True),
    )
    weighted = weigh(slope_all, curve_all, total)
    backs = windows(weighted, True)
    cot_part = jnp.zeros((pixel_count, kernel.shape[1]), jnp.float32)
    grads = []
    for tap in range(9):
        cot_part = cot_part + lax.dot_general(
            backs[tap], kernel[tap], (((1,), (1,)), ((), ())), preferred_element_type=jnp.float32
        )
        grads.append(
            lax.dot_general(
                acts[tap], weighted, (((0,), (0,)), ((), ())), preferred_element_type=jnp.float32
            )
        )
    kernel_product = jnp.stack(grads) / jnp.sqrt(jnp.float32(pixel_count))
    cotangent = lax.psum_scatter(cot_part, "filt", scatter_dimension=0, tiled=True).astype(
        jnp.bfloat16
    )
    return (cotangent, kernel_product)


def pieces_of(groups):
    for g, images in enumerate(groups):
        for strip in range(EIGHT):
            image, part = images[strip // STRIPS], strip % STRIPS
            for deep in range(DEEP):
                source = (image * HH + part * DEEP + deep) * WW
                yield g, strip, deep, source, (deep * len(groups) + g) * PIECE + strip


def sort_into(chunks, flat, sorted_, outs, cols):
    for groups, out in zip(chunks, outs):
        for _, _, _, source, target in pieces_of(groups):
            sorted_[pl.ds(target, WW, stride=EIGHT), :] = flat[pl.ds(source, WW), :]
        out[:, cols] = sorted_[pl.ds(0, out.shape[0]), :].astype(out.dtype)


def sort_kernel(chunks, x_ref, *refs):
    outs, (flat, sorted_) = refs[: len(chunks)], refs[len(chunks) :]
    blocks, each = x_ref.shape[0], x_ref.shape[1] // 2
    rows = flat.shape[0] // blocks
    for kind in range(2):
        for n in range(blocks):
            block = x_ref[n, kind * each : (kind + 1) * each, :].astype(jnp.float32)
            flat[n * rows : (n + 1) * rows, :] = block[:rows]
        sort_into(chunks, flat, sorted_, outs, pl.ds(kind * LANES, LANES))


def mix_kernel(chunks, a_ref, t_ref, *refs):
    outs, (flat, sorted_) = refs[: len(chunks)], refs[len(chunks) :]
    both = jnp.concatenate(
        [a_ref[...].astype(jnp.float32), t_ref[...].astype(jnp.float32)], axis=0
    )
    flat[...] = both.T
    sort_into(chunks, flat, sorted_, outs, pl.ds(0, LANES))


def sort_call(kernel, chunks, given, pixels, width):
    rows = [len(groups) * GROUP for groups in chunks]
    return pl.pallas_call(
        functools.partial(kernel, chunks),
        out_shape=[jax.ShapeDtypeStruct((r, width), given[0].dtype) for r in rows],
        scratch_shapes=[
            pltpu.VMEM((pixels, LANES), jnp.float32),
            pltpu.VMEM((max(rows), LANES), jnp.float32),
        ],
        compiler_params=PARAMS,
    )(*given)


def copy_all(copies):
    for copy in copies:
        copy.start()
    for copy in copies:
        copy.wait()


def build(x_ref, views, groups):
    width = x_ref.shape[1]
    strip = lax.broadcasted_iota(jnp.int32, (PIECE, width), 0) % STRIPS

    def put(at, block):
        at = pl.multiple_of(at, PIECE)
        none = jnp.zeros((EIGHT, width), jnp.float32)
        views[1, pl.ds(at, PIECE), :] = block.astype(jnp.bfloat16)
        before = jnp.concatenate([none, block[: PIECE - EIGHT]], axis=0)
        views[0, pl.ds(at, PIECE), :] = before.astype(jnp.bfloat16)
        after = jnp.concatenate([block[EIGHT:], none], axis=0)
        views[2, pl.ds(at, PIECE), :] = after.astype(jnp.bfloat16)

    def load(at):
        return x_ref[pl.ds(pl.multiple_of(at, PIECE), PIECE), :].astype(jnp.float32)

    def turn(block, by):
        return pltpu.roll(block.reshape(WW, EIGHT, width), by, 1).reshape(PIECE, width)

    @pl.loop(0, DEEP * groups)
    def _(n):
        put((groups + n) * PIECE, load(n * PIECE))

    @pl.loop(0, groups)
    def _(g):
        above = turn(load(((DEEP - 1) * groups + g) * PIECE), 1)
        put(g * PIECE, jnp.where(strip == 0, 0.0, above))
        below = turn(load(g * PIECE), EIGHT - 1)
        put(((DEEP + 1) * groups + g) * PIECE, jnp.where(strip == STRIPS - 1, 0.0, below))


def tap_rows(views, groups, row, col):
    start = row * (groups * PIECE)
    if not isinstance(row, int):
        start = pl.multiple_of(start, PIECE)
    return views[col, pl.ds(start, groups * GROUP), :]


def views_shape(groups, width):
    return pltpu.VMEM((3, (DEEP + 2) * groups * PIECE, width), jnp.bfloat16)


HALF, CHIP, PLACE, SHARDS = 0, 1, 2, 3


def tangent_kernel(groups, sources, slots, more, last, meta, *refs):
    count = len(slots)
    given = 1 + max(n for order in sources for n in order)
    shards = refs[:given]
    v_ref, w_ref = refs[given : given + 2]
    before = refs[given + 2] if more else None
    refs = refs[given + 2 + more :]
    if last:
        send_ref, keep_ref, xt_ref, x, xt, views, sem, *refs = refs
        acc, *refs = refs
    else:
        acc, xt_ref, x, xt, views, sem, *refs = refs
    away = pltpu.make_async_copy(xt, xt_ref, sem.at[count + 2])
    own = v_ref.shape[1] // len(sources)
    step = pl.program_id(0)

    @pl.when(step == 0)
    def _():
        fetch = []
        if count == 1:
            at = pl.ds(pl.multiple_of(meta[SHARDS + slots[0]] * own, own), own)
            for n, ref in enumerate((v_ref, w_ref)):
                to = refs[0].at[:, pl.ds(n * own, own), :]
                fetch.append(pltpu.make_async_copy(ref.at[:, at, :], to, sem.at[count + n]))
        for copy in fetch:
            copy.start()
        for z, order in enumerate(sources):

            @pl.when(meta[PLACE] == z)
            def _():
                copy_all(
                    [
                        pltpu.make_async_copy(
                            shards[n],
                            x.at[:, pl.ds(i * LANES, LANES)],
                            sem.at[i],
                        )
                        for i, n in enumerate(order)
                    ]
                )

        build(x, views, groups)
        for i in range(count):
            turned = x[:, i * LANES : (i + 1) * LANES].astype(jnp.float32).T
            xt[i * own : (i + 1) * own, :] = turned[:own].astype(jnp.bfloat16)
        away.start()
        for copy in fetch:
            copy.wait()

    if count == 1:
        lhs = [tap_rows(views, groups, row, col) for row in range(3) for col in range(3)]
        rhs = refs[0][...].reshape(9 * LANES, acc.shape[1])
    else:
        lhs, rhs = [], []
        for col in range(3):
            lhs.append(tap_rows(views, groups, step, col))
            for slot in slots:
                at = pl.ds(pl.multiple_of(meta[SHARDS + slot] * own, own), own)
                rhs += [v_ref[col, at, :], w_ref[col, at, :]]
        rhs = jnp.concatenate(rhs, axis=0)
    value = jnp.dot(jnp.concatenate(lhs, axis=1), rhs, preferred_element_type=jnp.float32)
    pl.when(step == pl.num_programs(0) - 1)(away.wait)
    if count == 1:
        acc[...] = before[...] + value if more else value
    elif more:
        acc[...] = value + jnp.where(step == 0, before[...], acc[...])
    else:
        acc[...] = jnp.where(step == 0, value, acc[...] + value)
    if last:
        pl.when(step == pl.num_programs(0) - 1)(
            functools.partial(halves, meta, acc, send_ref, keep_ref)
        )


def halves(meta, acc, send_ref, keep_ref):
    half, n = meta[HALF], acc.shape[0] // 2
    mine = pl.ds(pl.multiple_of(half * n, n), n)
    other = pl.ds(pl.multiple_of((1 - half) * n, n), n)
    send_ref[...] = acc[other, :].astype(jnp.bfloat16)
    keep_ref[...] = acc[mine, :]


def tangent(meta, shards, sources, slots, v, w, groups, before, last):
    more = before is not None
    rows = groups * GROUP
    channels, filters = w.shape[1:]
    count = len(slots)
    own = channels // len(sources)
    whole_block = pl.BlockSpec(memory_space=pl.ANY)
    row_block = pl.BlockSpec((3, channels, filters), lambda t, m: (t, 0, 0))

    def whole(*shape):
        return pl.BlockSpec(shape, lambda t, m: (0,) * len(shape))

    if last:
        outs = [(rows // 2, filters, jnp.bfloat16), (rows // 2, filters, jnp.float32)]
    else:
        outs = [(rows, filters, jnp.float32)]
    return pl.pallas_call(
        functools.partial(tangent_kernel, groups, sources, slots, more, last),
        grid_spec=pltpu.PrefetchScalarGridSpec(
            num_scalar_prefetch=1,
            grid=(1 if count == 1 else 3,),
            in_specs=[whole_block] * len(shards)
            + [whole_block if count == 1 else row_block] * 2
            + ([whole(rows, filters)] if more else []),
            out_specs=[whole(*o[:2]) for o in outs] + [pl.BlockSpec(memory_space=pltpu.HBM)],
            scratch_shapes=[
                pltpu.VMEM((rows, count * LANES), jnp.bfloat16),
                pltpu.VMEM((count * own, rows), jnp.bfloat16),
                views_shape(groups, count * LANES),
                pltpu.SemaphoreType.DMA((count + 3,)),
            ]
            + ([pltpu.VMEM((rows, filters), jnp.float32)] if last else [])
            + ([pltpu.VMEM((9, LANES, filters), jnp.bfloat16)] if count == 1 else []),
        ),
        out_shape=[jax.ShapeDtypeStruct(o[:2], o[2]) for o in outs]
        + [pltpu.HBM((count * own, rows), jnp.bfloat16)],
        cost_estimate=pl.CostEstimate(
            flops=18 * rows * count * LANES * filters,
            bytes_accessed=4 * w.size,
            transcendentals=0,
        ),
        name="tangent",
        compiler_params=PARAMS,
    )(meta, *shards, v, w, *([before] if more else []))


def split_kernel(meta, keep_ref, got_ref, mine_ref, *parts):
    for m in range(1 + len(parts)):
        at = pl.multiple_of((meta[CHIP] ^ m) * LANES, LANES)
        total = keep_ref[:, pl.ds(at, LANES)] + got_ref[:, pl.ds(at, LANES)].astype(jnp.float32)
        if m:
            parts[m - 1][...] = total.astype(jnp.bfloat16)
        else:
            mine_ref[...] = total


def split(meta, keep, got):
    rows, filters = keep.shape
    block = pl.BlockSpec((rows, filters), lambda t, m: (0, 0))
    out = pl.BlockSpec((rows, LANES), lambda t, m: (0, 0))
    kinds = [jnp.float32] + [jnp.bfloat16] * (filters // LANES - 1)
    return pl.pallas_call(
        split_kernel,
        grid_spec=pltpu.PrefetchScalarGridSpec(
            num_scalar_prefetch=1, grid=(1,), in_specs=[block] * 2, out_specs=[out] * len(kinds)
        ),
        out_shape=[jax.ShapeDtypeStruct((rows, LANES), kind) for kind in kinds],
        cost_estimate=pl.CostEstimate(
            flops=rows * filters, bytes_accessed=8 * keep.size, transcendentals=0
        ),
        name="split",
        compiler_params=PARAMS,
    )(meta, keep, got)


def gather_parts(meta, parts, x, sem):
    blocks, rows = len(parts) // 2, x.shape[0] // 2
    copies = []
    for n, part in enumerate(parts):
        half = meta[HALF] if n < blocks else 1 - meta[HALF]
        at = pl.multiple_of(half * rows, rows)
        lane = pl.multiple_of((meta[CHIP] ^ (n % blocks)) * LANES, LANES)
        to = x.at[pl.ds(at, rows), pl.ds(lane, LANES)]
        copies.append(pltpu.make_async_copy(part, to, sem.at[n]))
    copy_all(copies)


def cotangent_kernel(groups, places, meta, *refs):
    w_parts, (k_ref, out_ref, rows_ref, x, views, sem, acc, flat) = refs[:-8], refs[-8:]
    step = pl.program_id(0)
    keep = pltpu.make_async_copy(x, rows_ref, sem.at[len(w_parts)])

    @pl.when(step == 0)
    def _():
        gather_parts(meta, w_parts, x, sem)
        keep.start()
        build(x, views, len(groups))

    value = lax.dot_general(
        jnp.concatenate(
            [tap_rows(views, len(groups), 2 - step, 2 - col) for col in range(3)], axis=1
        ),
        jnp.concatenate([k_ref[col] for col in range(3)], axis=1),
        (((1,), (1,)), ((), ())),
        preferred_element_type=jnp.float32,
    )
    for n in range(acc.shape[0]):
        column = value[:, n * LANES : (n + 1) * LANES]
        acc[n] = jnp.where(step == 0, column, acc[n] + column)

    @pl.when(step == 2)
    def _():
        keep.wait()
        for n in range(acc.shape[0]):
            for g, strip, deep, _, row in pieces_of(groups):
                target = places(g, strip) + deep * WW
                flat[pl.ds(target, WW), :] = acc[n, pl.ds(row, WW, stride=EIGHT), :]
            out_ref[:, n * LANES : (n + 1) * LANES] = flat[...].astype(jnp.bfloat16)


def cotangent_part(meta, w_parts, groups, kernel, places):
    channels, filters = kernel.shape[1:]
    rows = 2 * w_parts[0].shape[0]
    return pl.pallas_call(
        functools.partial(cotangent_kernel, groups, places),
        grid_spec=pltpu.PrefetchScalarGridSpec(
            num_scalar_prefetch=1,
            grid=(3,),
            in_specs=[pl.BlockSpec(memory_space=pl.ANY)] * len(w_parts)
            + [pl.BlockSpec((3, channels, filters), lambda t, m: (t, 0, 0))],
            out_specs=[
                pl.BlockSpec((rows, channels), lambda t, m: (0, 0)),
                pl.BlockSpec(memory_space=pltpu.HBM),
            ],
            scratch_shapes=[
                pltpu.VMEM((rows, filters), jnp.bfloat16),
                views_shape(len(groups), filters),
                pltpu.SemaphoreType.DMA((len(w_parts) + 1,)),
                pltpu.VMEM((channels // LANES, rows, LANES), jnp.float32),
                pltpu.VMEM((rows, LANES), jnp.float32),
            ],
        ),
        out_shape=[
            jax.ShapeDtypeStruct((rows, channels), jnp.bfloat16),
            pltpu.HBM((rows, filters), jnp.bfloat16),
        ],
        cost_estimate=pl.CostEstimate(
            flops=18 * rows * channels * filters,
            bytes_accessed=18 * channels * filters,
            transcendentals=0,
        ),
        name="cotangent",
        compiler_params=PARAMS,
    )(meta, *w_parts, kernel)


def product_kernel(own, counts, sizes, scale, meta, *refs):
    chunks = len(counts)
    scratch = refs[-2 * chunks :]
    given, out_ref = refs[: -1 - 2 * chunks], refs[-1 - 2 * chunks]
    ends = [sum(sizes[: n + 1]) for n in range(chunks)]
    tap = pl.program_id(0)

    @pl.when(tap == 0)
    def _():
        for n, count in enumerate(counts):
            w_ref, *xts = given[ends[n] - sizes[n] : ends[n]]
            views, xt = scratch[2 * n : 2 * n + 2]
            build(w_ref, views, count)
            slot = 0
            for ref in xts:
                for row in range(0, ref.shape[0], own):
                    at = pl.multiple_of(meta[SHARDS + slot] * own, own)
                    xt[pl.ds(at, own), :] = ref[pl.ds(row, own), :]
                    slot += 1

    value = None
    for n, count in enumerate(counts):
        views, xt = scratch[2 * n : 2 * n + 2]
        term = jnp.dot(
            xt[...], tap_rows(views, count, 2 - tap // 3, 2 - lax.rem(tap, 3)), preferred_element_type=jnp.float32
        )
        value = term if value is None else value + term
    out_ref[0] = value * scale


def product_of(meta, chunks, counts, scale, channels, own):
    given = [array for chunk in chunks for array in chunk]
    total = sum(chunk[0].shape[0] for chunk in chunks)
    filters = chunks[0][0].shape[1]
    scratch = []
    for (w, *_), count in zip(chunks, counts):
        scratch += [views_shape(count, filters), pltpu.VMEM((channels, w.shape[0]), jnp.bfloat16)]
    return pl.pallas_call(
        functools.partial(product_kernel, own, counts, [len(chunk) for chunk in chunks], scale),
        grid_spec=pltpu.PrefetchScalarGridSpec(
            num_scalar_prefetch=1,
            grid=(9,),
            in_specs=[pl.BlockSpec(array.shape, lambda t, m: (0, 0)) for array in given],
            out_specs=pl.BlockSpec((1, channels, filters), lambda t, m: (t, 0, 0)),
            scratch_shapes=scratch,
        ),
        out_shape=jax.ShapeDtypeStruct((9, channels, filters), jnp.float32),
        cost_estimate=pl.CostEstimate(
            flops=18 * total * channels * filters,
            bytes_accessed=36 * channels * filters,
            transcendentals=0,
        ),
        name="product",
        compiler_params=PARAMS,
    )(meta, *given)


def pack_kernel(s_ref, c_ref, out_ref):
    rows = s_ref.shape[0]
    each = out_ref.shape[1] // 2
    for n in range(out_ref.shape[0]):
        cols = pl.ds(n // 2 * LANES, LANES)
        for kind, ref in enumerate((s_ref, c_ref)):
            out_ref[n, kind * each : kind * each + rows, :] = ref[:, cols]
            rest = jnp.zeros((each - rows, LANES), out_ref.dtype)
            out_ref[n, kind * each + rows : (kind + 1) * each, :] = rest


def pack(slope, curvature):
    rows, filters = slope.shape
    each = -(-rows // 16) * 16
    return pl.pallas_call(
        pack_kernel,
        out_shape=jax.ShapeDtypeStruct((2 * filters // LANES, 2 * each, LANES), slope.dtype),
        name="pack",
        compiler_params=PARAMS,
    )(slope, curvature)


def block_program(activations, act_tangent, kernel, kernel_tangent, slope, curvature):
    z, me = lax.axis_index("filt"), lax.axis_index("chan")
    depth, across = lax.axis_size("filt"), lax.axis_size("chan")
    half, chips = lax.rem(me, 2), across // 2
    pixels, own = activations.shape
    channels = kernel.shape[1]

    first, second, middle = [], [], []
    per = 2 * (pixels // (HH * WW)) // depth
    for a in range(0, depth, 2):
        at = a // 2 * per
        first += [(at, at + 1), (at + per - 2, at + per - 1)]
        second += [(at + 2, at + 3), (at + per - 4, at + per - 3)]
        middle.append(at + 4)
    second.append(tuple(middle))
    chunks = [second, first]

    orders, owners = [], []
    for place in range(depth):
        order, owner = [(0, 0)], [place]
        for step in range(1, depth):
            for link in range(2):
                shard = place + step if place % 2 == link else place - step
                if 0 <= shard < depth:
                    order.append((step, link))
                    owner.append(shard)
        orders.append(order)
        owners.append(owner)
    table = [
        [n % 2, n // 2, place] + owners[place]
        for place in range(depth)
        for n in range(across)
    ]
    meta = lax.dynamic_index_in_dim(
        jnp.asarray(table, jnp.int32), z * across + me, 0, keepdims=False
    )

    mixed = sort_call(mix_kernel, chunks, [activations.T, act_tangent.T], pixels, 2 * own)

    packed = pack(slope, curvature)
    packed = lax.all_to_all(packed, "chan", 0, 0, tiled=True)
    factors = sort_call(sort_kernel, chunks, [packed], pixels, 2 * LANES)

    def gathered(x):
        got = {(0, 0): x}
        last = [x, x]
        for step in range(1, depth):
            now = [None, None]
            for link in range(2):
                pairs = []
                for i in range(link, depth - 1, 2):
                    pairs += [(i, i + 1)] * (i >= step - 1) + [(i + 1, i)] * (i + 1 <= depth - step)
                if pairs:
                    now[link] = lax.ppermute(last[1 - link], "filt", pairs)
                    got[step, link] = now[link]
            last = now
        return got

    def swap(x, bit):
        return lax.ppermute(x, "chan", [(i, i ^ bit) for i in range(across)])

    def some(slots, c):
        names = sorted({order[slot] for order in orders for slot in slots})
        sources = [[names.index(order[slot]) for slot in slots] for order in orders]
        return [got[c][name] for name in names], sources

    def tangents(c):
        stages = [[0, 1], [2], [3]] if c == 0 else [[0, 1], [2, 3]]
        before, xts = None, []
        for n, slots in enumerate(stages):
            shards, sources = some(slots, c)
            *sums, xt = tangent(
                meta,
                shards,
                sources,
                slots,
                kernel_tangent,
                kernel,
                len(chunks[c]),
                before,
                n == len(stages) - 1,
            )
            before = sums[0]
            xts.append(xt)
        return sums, xts

    def exchange(send, keep):
        got = swap(send, 1)
        mine, *parts = split(meta, keep, got)
        for m, part in enumerate(parts):
            mine = mine + swap(part, 2 * (m + 1)).astype(jnp.float32)
        return mine

    def weighted(mine, factor):
        rows = mine.shape[0]
        factor = lax.dynamic_slice_in_dim(factor, half * rows, rows, axis=0)
        w = weigh(factor[:, :LANES], factor[:, LANES:], mine)
        parts = [w] + [swap(w, 2 * m) for m in range(1, chips)]
        return parts + [swap(part, 1) for part in parts]

    strip_rows = GROUP // EIGHT
    share = len(second) * GROUP // depth

    def place_first(g, strip):
        return g * GROUP + strip * strip_rows

    def place_second(g, strip):
        if g < depth:
            return g * share + strip * strip_rows
        place, rest = divmod(strip, EIGHT // depth)
        return place * share + GROUP + rest * strip_rows

    def spread(part):
        part = lax.all_to_all(
            part.reshape(depth, -1, channels), "filt", 0, 0, tiled=True
        ).astype(jnp.float32)
        total = part[0]
        for j in range(1, depth):
            total = total + part[j]
        return total.astype(jnp.bfloat16)

    got = [gathered(x) for x in mixed]
    sums, xts = zip(*[tangents(c) for c in range(2)])
    mine = [exchange(*sums[c]) for c in range(2)]
    w = [weighted(mine[c], factors[c]) for c in range(2)]
    cots, whole = [], []
    for c, place in enumerate((place_second, place_first)):
        part, rows = cotangent_part(meta, w[c], chunks[c], kernel, place)
        cots.append(spread(part))
        whole.append(rows)
    scale = float(1.0 / (float(pixels) ** 0.5))
    product = product_of(
        meta,
        [(whole[c], *xts[c]) for c in range(2)],
        [len(groups) for groups in chunks],
        scale,
        channels,
        own,
    )
    inner, outer = cots
    main, edge = inner[:GROUP], inner[GROUP:]
    result = jnp.where(
        lax.rem(z, 2) == 0,
        jnp.concatenate([outer, main, edge], axis=0),
        jnp.concatenate([edge, main, outer], axis=0),
    )
    return (result, product)


def block_device(*args):
    return block_program(*args)


def fits(mesh, pixels, channels, filters):
    depth, across = mesh.shape["filt"], mesh.shape["chan"]
    images = pixels // (HH * WW)
    return (
        depth == 2 * PAIR
        and 2 * images == 9 * depth
        and across == 8
        and 2 * channels == LANES * across * depth
        and filters == LANES * (across // 2) * depth
    )


def solution(mesh):
    in_specs = (
        P(None, ("chan", "filt")),
        P(None, ("chan", "filt")),
        P(None, "chan", "filt"),
        P(None, "chan", "filt"),
        P("chan", "filt"),
        P("chan", "filt"),
    )

    def program(*args):
        pixels, channels = args[0].shape
        body = block_device if fits(mesh, pixels, channels, args[2].shape[2]) else any_device
        return jax.shard_map(
            body,
            mesh=mesh,
            in_specs=in_specs,
            out_specs=(P("filt", "chan"), P(None, "chan", "filt")),
            check_vma=False,
        )(*args)

    return program
```

```python
import functools

import jax
import jax.numpy as jnp
from jax import lax
from jax.experimental import pallas as pl
from jax.experimental.pallas import tpu as pltpu
from jax.sharding import PartitionSpec as P


HH = 12
WW = 12
LANES = 128
STRIPS = 4
DEEP = HH // STRIPS
PAIR = 2
EIGHT = PAIR * STRIPS
PIECE = WW * EIGHT
GROUP = DEEP * PIECE

INNER = 1
PARAMS = pltpu.CompilerParams(vmem_limit_bytes=28 << 20)


def windows(flat, flip):
    width = flat.shape[-1]
    image = flat.reshape(-1, HH, WW, width)
    padded = jnp.pad(image, ((0, 0), (1, 1), (1, 1), (0, 0)))
    result = []
    for row_tap in range(3):
        for col_tap in range(3):
            top = 2 - row_tap if flip else row_tap
            left = 2 - col_tap if flip else col_tap
            result.append(padded[:, top : top + HH, left : left + WW, :].reshape(-1, width))
    return result


def weigh(slope, curvature, tangent):
    slope_f = slope.astype(jnp.float32)
    return (slope_f * slope_f * curvature.astype(jnp.float32) * tangent).astype(jnp.bfloat16)


def any_device(activations, act_tangent, kernel, kernel_tangent, slope, curvature):
    acts_block, tans_block = (
        lax.all_gather(activations, "filt", axis=1, tiled=True),
        lax.all_gather(act_tangent, "filt", axis=1, tiled=True),
    )
    acts = windows(acts_block, False)
    tans = windows(tans_block, False)
    pixel_count = acts_block.shape[0]
    partial_value = jnp.zeros((pixel_count, kernel.shape[2]), jnp.float32)
    for tap in range(9):
        partial_value = partial_value + jnp.dot(
            tans[tap], kernel[tap], preferred_element_type=jnp.float32
        )
        partial_value = partial_value + jnp.dot(
            acts[tap], kernel_tangent[tap], preferred_element_type=jnp.float32
        )
    total = lax.psum(partial_value, "chan")
    slope_all, curve_all = (
        lax.all_gather(slope, "chan", axis=0, tiled=True),
        lax.all_gather(curvature, "chan", axis=0, tiled=True),
    )
    weighted = weigh(slope_all, curve_all, total)
    backs = windows(weighted, True)
    cot_part = jnp.zeros((pixel_count, kernel.shape[1]), jnp.float32)
    grads = []
    for tap in range(9):
        cot_part = cot_part + lax.dot_general(
            backs[tap], kernel[tap], (((1,), (1,)), ((), ())), preferred_element_type=jnp.float32
        )
        grads.append(
            lax.dot_general(
                acts[tap], weighted, (((0,), (0,)), ((), ())), preferred_element_type=jnp.float32
            )
        )
    kernel_product = jnp.stack(grads) / jnp.sqrt(jnp.float32(pixel_count))
    cotangent = lax.psum_scatter(cot_part, "filt", scatter_dimension=0, tiled=True).astype(
        jnp.bfloat16
    )
    return (cotangent, kernel_product)


def pieces_of(groups):
    for g, images in enumerate(groups):
        for strip in range(EIGHT):
            image, part = images[strip // STRIPS], strip % STRIPS
            for deep in range(DEEP):
                source = (image * HH + part * DEEP + deep) * WW
                yield g, strip, deep, source, (deep * len(groups) + g) * PIECE + strip


def sort_into(chunks, flat, sorted_, outs, cols):
    for groups, out in zip(chunks, outs):
        for _, _, _, source, target in pieces_of(groups):
            sorted_[pl.ds(target, WW, stride=EIGHT), :] = flat[pl.ds(source, WW), :]
        out[:, cols] = sorted_[pl.ds(0, out.shape[0]), :].astype(out.dtype)


def sort_kernel(chunks, x_ref, *refs):
    outs, (flat, sorted_) = refs[: len(chunks)], refs[len(chunks) :]
    blocks, each = x_ref.shape[0], x_ref.shape[1] // 2
    rows = flat.shape[0] // blocks
    for kind in range(2):
        for n in range(blocks):
            block = x_ref[n, kind * each : (kind + 1) * each, :].astype(jnp.float32)
            flat[n * rows : (n + 1) * rows, :] = block[:rows]
        sort_into(chunks, flat, sorted_, outs, pl.ds(kind * LANES, LANES))


def mix_kernel(chunks, a_ref, t_ref, *refs):
    outs, (flat, sorted_) = refs[: len(chunks)], refs[len(chunks) :]
    both = jnp.concatenate(
        [a_ref[...].astype(jnp.float32), t_ref[...].astype(jnp.float32)], axis=0
    )
    flat[...] = both.T
    sort_into(chunks, flat, sorted_, outs, pl.ds(0, LANES))


def sort_call(kernel, chunks, given, pixels, width):
    rows = [len(groups) * GROUP for groups in chunks]
    return pl.pallas_call(
        functools.partial(kernel, chunks),
        out_shape=[jax.ShapeDtypeStruct((r, width), given[0].dtype) for r in rows],
        scratch_shapes=[
            pltpu.VMEM((pixels, LANES), jnp.float32),
            pltpu.VMEM((max(rows), LANES), jnp.float32),
        ],
        compiler_params=PARAMS,
    )(*given)


def copy_all(copies):
    for copy in copies:
        copy.start()
    for copy in copies:
        copy.wait()


def build(x_ref, views, groups):
    width = x_ref.shape[1]
    strip = lax.broadcasted_iota(jnp.int32, (PIECE, width), 0) % STRIPS

    def put(at, block):
        at = pl.multiple_of(at, PIECE)
        none = jnp.zeros((EIGHT, width), jnp.float32)
        views[1, pl.ds(at, PIECE), :] = block.astype(jnp.bfloat16)
        before = jnp.concatenate([none, block[: PIECE - EIGHT]], axis=0)
        views[0, pl.ds(at, PIECE), :] = before.astype(jnp.bfloat16)
        after = jnp.concatenate([block[EIGHT:], none], axis=0)
        views[2, pl.ds(at, PIECE), :] = after.astype(jnp.bfloat16)

    def load(at):
        return x_ref[pl.ds(pl.multiple_of(at, PIECE), PIECE), :].astype(jnp.float32)

    def turn(block, by):
        return pltpu.roll(block.reshape(WW, EIGHT, width), by, 1).reshape(PIECE, width)

    @pl.loop(0, DEEP * groups)
    def _(n):
        put((groups + n) * PIECE, load(n * PIECE))

    @pl.loop(0, groups)
    def _(g):
        above = turn(load(((DEEP - 1) * groups + g) * PIECE), 1)
        put(g * PIECE, jnp.where(strip == 0, 0.0, above))
        below = turn(load(g * PIECE), EIGHT - 1)
        put(((DEEP + 1) * groups + g) * PIECE, jnp.where(strip == STRIPS - 1, 0.0, below))


def tap_rows(views, groups, row, col):
    start = row * (groups * PIECE)
    if not isinstance(row, int):
        start = pl.multiple_of(start, PIECE)
    return views[col, pl.ds(start, groups * GROUP), :]


def views_shape(groups, width):
    return pltpu.VMEM((3, (DEEP + 2) * groups * PIECE, width), jnp.bfloat16)


HALF, CHIP, PLACE, SHARDS = 0, 1, 2, 3


def tangent_kernel(groups, sources, slots, more, last, meta, *refs):
    count = len(slots)
    given = 1 + max(n for order in sources for n in order)
    shards = refs[:given]
    v_ref, w_ref = refs[given : given + 2]
    before = refs[given + 2] if more else None
    refs = refs[given + 2 + more :]
    if last:
        send_ref, keep_ref, xt_ref, x, xt, views, sem, *refs = refs
        acc, *refs = refs
    else:
        acc, xt_ref, x, xt, views, sem, *refs = refs
    away = pltpu.make_async_copy(xt, xt_ref, sem.at[count + 2])
    own = v_ref.shape[1] // len(sources)
    step = pl.program_id(0)

    @pl.when(step == 0)
    def _():
        fetch = []
        if count == 1:
            at = pl.ds(pl.multiple_of(meta[SHARDS + slots[0]] * own, own), own)
            for n, ref in enumerate((v_ref, w_ref)):
                to = refs[0].at[:, pl.ds(n * own, own), :]
                fetch.append(pltpu.make_async_copy(ref.at[:, at, :], to, sem.at[count + n]))
        for copy in fetch:
            copy.start()
        for z, order in enumerate(sources):

            @pl.when(meta[PLACE] == z)
            def _():
                copy_all(
                    [
                        pltpu.make_async_copy(
                            shards[n],
                            x.at[:, pl.ds(i * LANES, LANES)],
                            sem.at[i],
                        )
                        for i, n in enumerate(order)
                    ]
                )

        build(x, views, groups)
        for i in range(count):
            turned = x[:, i * LANES : (i + 1) * LANES].astype(jnp.float32).T
            xt[i * own : (i + 1) * own, :] = turned[:own].astype(jnp.bfloat16)
        away.start()
        for copy in fetch:
            copy.wait()

    if count == 1:
        lhs = [tap_rows(views, groups, row, col) for row in range(3) for col in range(3)]
        rhs = refs[0][...].reshape(9 * LANES, acc.shape[1])
    else:
        lhs, rhs = [], []
        for col in range(3):
            lhs.append(tap_rows(views, groups, step, col))
            for slot in slots:
                at = pl.ds(pl.multiple_of(meta[SHARDS + slot] * own, own), own)
                rhs += [v_ref[col, at, :], w_ref[col, at, :]]
        rhs = jnp.concatenate(rhs, axis=0)
    value = jnp.dot(jnp.concatenate(lhs, axis=1), rhs, preferred_element_type=jnp.float32)
    pl.when(step == pl.num_programs(0) - 1)(away.wait)
    if count == 1:
        acc[...] = before[...] + value if more else value
    elif more:
        acc[...] = value + jnp.where(step == 0, before[...], acc[...])
    else:
        acc[...] = jnp.where(step == 0, value, acc[...] + value)
    if last:
        pl.when(step == pl.num_programs(0) - 1)(
            functools.partial(halves, meta, acc, send_ref, keep_ref)
        )


def halves(meta, acc, send_ref, keep_ref):
    half, n = meta[HALF], acc.shape[0] // 2
    mine = pl.ds(pl.multiple_of(half * n, n), n)
    other = pl.ds(pl.multiple_of((1 - half) * n, n), n)
    send_ref[...] = acc[other, :].astype(jnp.bfloat16)
    keep_ref[...] = acc[mine, :]


def tangent(meta, shards, sources, slots, v, w, groups, before, last):
    more = before is not None
    rows = groups * GROUP
    channels, filters = w.shape[1:]
    count = len(slots)
    own = channels // len(sources)
    whole_block = pl.BlockSpec(memory_space=pl.ANY)
    row_block = pl.BlockSpec((3, channels, filters), lambda t, m: (t, 0, 0))

    def whole(*shape):
        return pl.BlockSpec(shape, lambda t, m: (0,) * len(shape))

    hbm = pl.BlockSpec(memory_space=pltpu.HBM)
    if last:
        out_specs = [whole(rows // 2, filters)] * 2
        outs = [
            jax.ShapeDtypeStruct((rows // 2, filters), jnp.bfloat16),
            jax.ShapeDtypeStruct((rows // 2, filters), jnp.float32),
        ]
    else:
        out_specs = [whole(rows, filters)]
        outs = [jax.ShapeDtypeStruct((rows, filters), jnp.float32)]
    return pl.pallas_call(
        functools.partial(tangent_kernel, groups, sources, slots, more, last),
        grid_spec=pltpu.PrefetchScalarGridSpec(
            num_scalar_prefetch=1,
            grid=(1 if count == 1 else 3,),
            in_specs=[whole_block] * len(shards)
            + [whole_block if count == 1 else row_block] * 2
            + ([whole(rows, filters)] if more else []),
            out_specs=out_specs + [hbm],
            scratch_shapes=[
                pltpu.VMEM((rows, count * LANES), jnp.bfloat16),
                pltpu.VMEM((count * own, rows), jnp.bfloat16),
                views_shape(groups, count * LANES),
                pltpu.SemaphoreType.DMA((count + 3,)),
            ]
            + ([pltpu.VMEM((rows, filters), jnp.float32)] if last else [])
            + ([pltpu.VMEM((9, LANES, filters), jnp.bfloat16)] if count == 1 else []),
        ),
        out_shape=outs + [pltpu.HBM((count * own, rows), jnp.bfloat16)],
        cost_estimate=pl.CostEstimate(
            flops=18 * rows * count * LANES * filters,
            bytes_accessed=4 * w.size,
            transcendentals=0,
        ),
        name="tangent",
        compiler_params=PARAMS,
    )(meta, *shards, v, w, *([before] if more else []))


def split_kernel(meta, keep_ref, got_ref, mine_ref, *parts):
    for m in range(1 + len(parts)):
        at = pl.multiple_of((meta[CHIP] ^ m) * LANES, LANES)
        total = keep_ref[:, pl.ds(at, LANES)] + got_ref[:, pl.ds(at, LANES)].astype(jnp.float32)
        if m:
            parts[m - 1][...] = total.astype(jnp.bfloat16)
        else:
            mine_ref[...] = total


def split(meta, keep, got):
    rows, filters = keep.shape
    block = pl.BlockSpec((rows, filters), lambda t, m: (0, 0))
    out = pl.BlockSpec((rows, LANES), lambda t, m: (0, 0))
    kinds = [jnp.float32] + [jnp.bfloat16] * (filters // LANES - 1)
    return pl.pallas_call(
        split_kernel,
        grid_spec=pltpu.PrefetchScalarGridSpec(
            num_scalar_prefetch=1, grid=(1,), in_specs=[block] * 2, out_specs=[out] * len(kinds)
        ),
        out_shape=[jax.ShapeDtypeStruct((rows, LANES), kind) for kind in kinds],
        cost_estimate=pl.CostEstimate(
            flops=rows * filters, bytes_accessed=8 * keep.size, transcendentals=0
        ),
        name="split",
        compiler_params=PARAMS,
    )(meta, keep, got)


def gather_parts(meta, parts, x, sem):
    blocks, rows = len(parts) // 2, x.shape[0] // 2
    copies = []
    for n, part in enumerate(parts):
        half = meta[HALF] if n < blocks else 1 - meta[HALF]
        at = pl.multiple_of(half * rows, rows)
        lane = pl.multiple_of((meta[CHIP] ^ (n % blocks)) * LANES, LANES)
        to = x.at[pl.ds(at, rows), pl.ds(lane, LANES)]
        copies.append(pltpu.make_async_copy(part, to, sem.at[n]))
    copy_all(copies)


def cotangent_kernel(groups, places, parts, meta, *refs):
    outs = refs[-6 - parts : -6]
    w_parts, k_ref = refs[: -7 - parts], refs[-7 - parts]
    rows_ref, x, views, sem, acc, flat = refs[-6:]
    step = pl.program_id(0)
    keep = pltpu.make_async_copy(x, rows_ref, sem.at[len(w_parts)])

    @pl.when(step == 0)
    def _():
        gather_parts(meta, w_parts, x, sem)
        keep.start()
        build(x, views, len(groups))

    value = lax.dot_general(
        jnp.concatenate(
            [tap_rows(views, len(groups), 2 - step, 2 - col) for col in range(3)], axis=1
        ),
        jnp.concatenate([k_ref[col] for col in range(3)], axis=1),
        (((1,), (1,)), ((), ())),
        preferred_element_type=jnp.float32,
    )
    for n in range(acc.shape[0]):
        column = value[:, n * LANES : (n + 1) * LANES]
        acc[n] = jnp.where(step == 0, column, acc[n] + column)

    @pl.when(step == 2)
    def _():
        keep.wait()
        for n in range(acc.shape[0]):
            for g, strip, deep, _, row in pieces_of(groups):
                target = places[g, strip] + deep * WW
                flat[pl.ds(target, WW), :] = acc[n, pl.ds(row, WW, stride=EIGHT), :]
            share = flat.shape[0] // parts
            for m, out in enumerate(outs):
                at = pl.multiple_of((meta[PLACE] ^ m) * share, share)
                cols = pl.ds(n * LANES, LANES)
                out[:, cols] = flat[pl.ds(at, share), :].astype(out.dtype)


def cotangent_part(meta, w_parts, groups, kernel, places, parts):
    channels, filters = kernel.shape[1:]
    rows = 2 * w_parts[0].shape[0]
    return pl.pallas_call(
        functools.partial(cotangent_kernel, groups, places, parts),
        grid_spec=pltpu.PrefetchScalarGridSpec(
            num_scalar_prefetch=1,
            grid=(3,),
            in_specs=[pl.BlockSpec(memory_space=pl.ANY)] * len(w_parts)
            + [pl.BlockSpec((3, channels, filters), lambda t, m: (t, 0, 0))],
            out_specs=[pl.BlockSpec((rows // parts, channels), lambda t, m: (0, 0))] * parts
            + [pl.BlockSpec(memory_space=pltpu.HBM)],
            scratch_shapes=[
                pltpu.VMEM((rows, filters), jnp.bfloat16),
                views_shape(len(groups), filters),
                pltpu.SemaphoreType.DMA((len(w_parts) + 1,)),
                pltpu.VMEM((channels // LANES, rows, LANES), jnp.float32),
                pltpu.VMEM((rows, LANES), jnp.float32),
            ],
        ),
        out_shape=[
            jax.ShapeDtypeStruct((rows // parts, channels), jnp.bfloat16 if m else jnp.float32)
            for m in range(parts)
        ]
        + [pltpu.HBM((rows, filters), jnp.bfloat16)],
        cost_estimate=pl.CostEstimate(
            flops=18 * rows * channels * filters,
            bytes_accessed=18 * channels * filters,
            transcendentals=0,
        ),
        name="cotangent",
        compiler_params=PARAMS,
    )(meta, *w_parts, kernel)


def product_kernel(own, counts, sizes, scale, meta, *refs):
    chunks = len(counts)
    scratch = refs[-2 * chunks :]
    given, out_ref = refs[: -1 - 2 * chunks], refs[-1 - 2 * chunks]
    ends = [sum(sizes[: n + 1]) for n in range(chunks)]
    tap = pl.program_id(0)

    @pl.when(tap == 0)
    def _():
        for n, count in enumerate(counts):
            w_ref, *xts = given[ends[n] - sizes[n] : ends[n]]
            views, xt = scratch[2 * n : 2 * n + 2]
            build(w_ref, views, count)
            slot = 0
            for ref in xts:
                for row in range(0, ref.shape[0], own):
                    at = pl.multiple_of(meta[SHARDS + slot] * own, own)
                    xt[pl.ds(at, own), :] = ref[pl.ds(row, own), :]
                    slot += 1

    value = None
    for n, count in enumerate(counts):
        views, xt = scratch[2 * n : 2 * n + 2]
        term = jnp.dot(
            xt[...], tap_rows(views, count, 2 - tap // 3, 2 - lax.rem(tap, 3)), preferred_element_type=jnp.float32
        )
        value = term if value is None else value + term
    out_ref[0] = value * scale


def product_of(meta, chunks, counts, scale, channels, own):
    given = [array for chunk in chunks for array in chunk]
    total = sum(chunk[0].shape[0] for chunk in chunks)
    filters = chunks[0][0].shape[1]
    scratch = []
    for (w, *_), count in zip(chunks, counts):
        scratch += [views_shape(count, filters), pltpu.VMEM((channels, w.shape[0]), jnp.bfloat16)]
    return pl.pallas_call(
        functools.partial(product_kernel, own, counts, [len(chunk) for chunk in chunks], scale),
        grid_spec=pltpu.PrefetchScalarGridSpec(
            num_scalar_prefetch=1,
            grid=(9,),
            in_specs=[pl.BlockSpec(array.shape, lambda t, m: (0, 0)) for array in given],
            out_specs=pl.BlockSpec((1, channels, filters), lambda t, m: (t, 0, 0)),
            scratch_shapes=scratch,
        ),
        out_shape=jax.ShapeDtypeStruct((9, channels, filters), jnp.float32),
        cost_estimate=pl.CostEstimate(
            flops=18 * total * channels * filters,
            bytes_accessed=36 * channels * filters,
            transcendentals=0,
        ),
        name="product",
        compiler_params=PARAMS,
    )(meta, *given)


def pack_kernel(s_ref, c_ref, out_ref):
    rows = s_ref.shape[0]
    each = out_ref.shape[1] // 2
    for n in range(out_ref.shape[0]):
        cols = pl.ds(n // 2 * LANES, LANES)
        for kind, ref in enumerate((s_ref, c_ref)):
            out_ref[n, kind * each : kind * each + rows, :] = ref[:, cols]
            rest = jnp.zeros((each - rows, LANES), out_ref.dtype)
            out_ref[n, kind * each + rows : (kind + 1) * each, :] = rest


def pack(slope, curvature):
    rows, filters = slope.shape
    each = -(-rows // 16) * 16
    return pl.pallas_call(
        pack_kernel,
        out_shape=jax.ShapeDtypeStruct((2 * filters // LANES, 2 * each, LANES), slope.dtype),
        name="pack",
        compiler_params=PARAMS,
    )(slope, curvature)


def block_program(activations, act_tangent, kernel, kernel_tangent, slope, curvature):
    z, me = lax.axis_index("filt"), lax.axis_index("chan")
    depth, across = lax.axis_size("filt"), lax.axis_size("chan")
    half, chips = lax.rem(me, 2), across // 2
    pixels, own = activations.shape
    channels = kernel.shape[1]

    per = 2 * (pixels // (HH * WW)) // depth
    outer, inner = [], []
    for image in range(per * depth // 2):
        (inner if abs(image % per - per // 2) <= INNER else outer).append(image)
    chunks = [list(zip(images[::PAIR], images[1::PAIR])) for images in (outer, inner)]

    orders, owners = [], []
    for place in range(depth):
        order, owner = [(0, 0)], [place]
        for step in range(1, depth):
            for link in range(2):
                shard = place + step if place % 2 == link else place - step
                if 0 <= shard < depth:
                    order.append((step, link))
                    owner.append(shard)
        orders.append(order)
        owners.append(owner)
    table = [
        [n % 2, n // 2, place] + owners[place]
        for place in range(depth)
        for n in range(across)
    ]
    meta = lax.dynamic_index_in_dim(
        jnp.asarray(table, jnp.int32), z * across + me, 0, keepdims=False
    )

    mixed = sort_call(mix_kernel, chunks, [activations.T, act_tangent.T], pixels, 2 * own)

    packed = pack(slope, curvature)
    packed = lax.all_to_all(packed, "chan", 0, 0, tiled=True)
    factors = sort_call(sort_kernel, chunks, [packed], pixels, 2 * LANES)

    def gathered(x):
        got = {(0, 0): x}
        last = [x, x]
        for step in range(1, depth):
            now = [None, None]
            for link in range(2):
                pairs = []
                for i in range(link, depth - 1, 2):
                    pairs += [(i, i + 1)] * (i >= step - 1) + [(i + 1, i)] * (i + 1 <= depth - step)
                if pairs:
                    now[link] = lax.ppermute(last[1 - link], "filt", pairs)
                    got[step, link] = now[link]
            last = now
        return got

    def swap(x, bit):
        return lax.ppermute(x, "chan", [(i, i ^ bit) for i in range(across)])

    def some(slots, c):
        names = sorted({order[slot] for order in orders for slot in slots})
        sources = [[names.index(order[slot]) for slot in slots] for order in orders]
        return [got[c][name] for name in names], sources

    def tangents(c):
        stages = [[0, 1], [2], [3]] if c == 0 else [[0, 1], [2, 3]]
        before, xts = None, []
        for n, slots in enumerate(stages):
            shards, sources = some(slots, c)
            *sums, xt = tangent(
                meta,
                shards,
                sources,
                slots,
                kernel_tangent,
                kernel,
                len(chunks[c]),
                before,
                n == len(stages) - 1,
            )
            before = sums[0]
            xts.append(xt)
        return sums, xts

    def exchange(send, keep):
        got = swap(send, 1)
        mine, *parts = split(meta, keep, got)
        for m, part in enumerate(parts):
            mine = mine + swap(part, 2 * (m + 1)).astype(jnp.float32)
        return mine

    def weighted(mine, factor):
        rows = mine.shape[0]
        factor = lax.dynamic_slice_in_dim(factor, half * rows, rows, axis=0)
        w = weigh(factor[:, :LANES], factor[:, LANES:], mine)
        parts = [w] + [swap(w, 2 * m) for m in range(1, chips)]
        parts += [swap(part, 1) for part in parts]
        return [pltpu.with_memory_space_constraint(part, pltpu.HBM) for part in parts]

    def places_of(groups):
        strip_rows = GROUP // EIGHT
        sources = {}
        for g, images in enumerate(groups):
            for strip in range(EIGHT):
                row = images[strip // STRIPS] * HH * WW + strip % STRIPS * strip_rows
                sources[row] = (g, strip)
        return {sources[row]: n * strip_rows for n, row in enumerate(sorted(sources))}

    def spread(own_part, parts):
        total = own_part
        for m, part in enumerate(parts):
            part = lax.ppermute(part, "filt", [(i, i ^ (m + 1)) for i in range(depth)])
            total = total + part.astype(jnp.float32)
        return total.astype(jnp.bfloat16)

    got = [gathered(x) for x in mixed]
    sums, xts = zip(*[tangents(c) for c in range(2)])
    mine = [exchange(*sums[c]) for c in range(2)]
    w = [weighted(mine[c], factors[c]) for c in range(2)]
    cots, whole = [], []
    for c, place in enumerate([places_of(groups) for groups in chunks]):
        own_part, *parts, rows = cotangent_part(meta, w[c], chunks[c], kernel, place, depth)
        cots.append(spread(own_part, parts))
        whole.append(rows)
    scale = float(1.0 / (float(pixels) ** 0.5))
    product = product_of(
        meta,
        [(whole[c], *xts[c]) for c in range(2)],
        [len(groups) for groups in chunks],
        scale,
        channels,
        own,
    )
    result = jnp.where(
        lax.rem(z, 2) == 0, jnp.concatenate(cots, axis=0), jnp.concatenate(cots[::-1], axis=0)
    )
    return (result, product)


def block_device(*args):
    return block_program(*args)


def fits(mesh, pixels, channels, filters):
    depth, across = mesh.shape["filt"], mesh.shape["chan"]
    images = pixels // (HH * WW)
    return (
        depth == 2 * PAIR
        and 2 * images == 9 * depth
        and across == 8
        and 2 * channels == LANES * across * depth
        and filters == LANES * (across // 2) * depth
    )


def solution(mesh):
    in_specs = (
        P(None, ("chan", "filt")),
        P(None, ("chan", "filt")),
        P(None, "chan", "filt"),
        P(None, "chan", "filt"),
        P("chan", "filt"),
        P("chan", "filt"),
    )

    def program(*args):
        pixels, channels = args[0].shape
        body = block_device if fits(mesh, pixels, channels, args[2].shape[2]) else any_device
        return jax.shard_map(
            body,
            mesh=mesh,
            in_specs=in_specs,
            out_specs=(P("filt", "chan"), P(None, "chan", "filt")),
            check_vma=False,
        )(*args)

    return program
```

```python
import functools

import jax
import jax.numpy as jnp
from jax import lax
from jax.experimental import pallas as pl
from jax.experimental.pallas import tpu as pltpu
from jax.sharding import PartitionSpec as P


HH = 12
WW = 12
LANES = 128
STRIPS = 4
DEEP = HH // STRIPS
PAIR = 2
EIGHT = PAIR * STRIPS
PIECE = WW * EIGHT
GROUP = DEEP * PIECE

INNER = 1
PARAMS = pltpu.CompilerParams(vmem_limit_bytes=28 << 20)


def windows(flat, flip):
    width = flat.shape[-1]
    image = flat.reshape(-1, HH, WW, width)
    padded = jnp.pad(image, ((0, 0), (1, 1), (1, 1), (0, 0)))
    result = []
    for row_tap in range(3):
        for col_tap in range(3):
            top = 2 - row_tap if flip else row_tap
            left = 2 - col_tap if flip else col_tap
            result.append(padded[:, top : top + HH, left : left + WW, :].reshape(-1, width))
    return result


def weigh(slope, curvature, tangent):
    slope_f = slope.astype(jnp.float32)
    return (slope_f * slope_f * curvature.astype(jnp.float32) * tangent).astype(jnp.bfloat16)


def any_device(activations, act_tangent, kernel, kernel_tangent, slope, curvature):
    acts_block, tans_block = (
        lax.all_gather(activations, "filt", axis=1, tiled=True),
        lax.all_gather(act_tangent, "filt", axis=1, tiled=True),
    )
    acts = windows(acts_block, False)
    tans = windows(tans_block, False)
    pixel_count = acts_block.shape[0]
    partial_value = jnp.zeros((pixel_count, kernel.shape[2]), jnp.float32)
    for tap in range(9):
        partial_value = partial_value + jnp.dot(
            tans[tap], kernel[tap], preferred_element_type=jnp.float32
        )
        partial_value = partial_value + jnp.dot(
            acts[tap], kernel_tangent[tap], preferred_element_type=jnp.float32
        )
    total = lax.psum(partial_value, "chan")
    slope_all, curve_all = (
        lax.all_gather(slope, "chan", axis=0, tiled=True),
        lax.all_gather(curvature, "chan", axis=0, tiled=True),
    )
    weighted = weigh(slope_all, curve_all, total)
    backs = windows(weighted, True)
    cot_part = jnp.zeros((pixel_count, kernel.shape[1]), jnp.float32)
    grads = []
    for tap in range(9):
        cot_part = cot_part + lax.dot_general(
            backs[tap], kernel[tap], (((1,), (1,)), ((), ())), preferred_element_type=jnp.float32
        )
        grads.append(
            lax.dot_general(
                acts[tap], weighted, (((0,), (0,)), ((), ())), preferred_element_type=jnp.float32
            )
        )
    kernel_product = jnp.stack(grads) / jnp.sqrt(jnp.float32(pixel_count))
    cotangent = lax.psum_scatter(cot_part, "filt", scatter_dimension=0, tiled=True).astype(
        jnp.bfloat16
    )
    return (cotangent, kernel_product)


def pieces_of(groups):
    for g, images in enumerate(groups):
        for strip in range(EIGHT):
            image, part = images[strip // STRIPS], strip % STRIPS
            for deep in range(DEEP):
                source = (image * HH + part * DEEP + deep) * WW
                yield g, strip, deep, source, (deep * len(groups) + g) * PIECE + strip


def sort_into(chunks, flat, sorted_, outs, cols):
    for groups, out in zip(chunks, outs):
        for _, _, _, source, target in pieces_of(groups):
            sorted_[pl.ds(target, WW, stride=EIGHT), :] = flat[pl.ds(source, WW), :]
        out[:, cols] = sorted_[pl.ds(0, out.shape[0]), :].astype(out.dtype)


def sort_kernel(chunks, x_ref, *refs):
    outs, (flat, sorted_) = refs[: len(chunks)], refs[len(chunks) :]
    blocks, each = x_ref.shape[0], x_ref.shape[1] // 2
    rows = flat.shape[0] // blocks
    for kind in range(2):
        for n in range(blocks):
            block = x_ref[n, kind * each : (kind + 1) * each, :].astype(jnp.float32)
            flat[n * rows : (n + 1) * rows, :] = block[:rows]
        sort_into(chunks, flat, sorted_, outs, pl.ds(kind * LANES, LANES))


def mix_kernel(chunks, a_ref, t_ref, *refs):
    outs, (flat, sorted_) = refs[: len(chunks)], refs[len(chunks) :]
    both = jnp.concatenate(
        [a_ref[...].astype(jnp.float32), t_ref[...].astype(jnp.float32)], axis=0
    )
    flat[...] = both.T
    sort_into(chunks, flat, sorted_, outs, pl.ds(0, LANES))


def sort_call(kernel, chunks, given, pixels, width):
    rows = [len(groups) * GROUP for groups in chunks]
    return pl.pallas_call(
        functools.partial(kernel, chunks),
        out_shape=[jax.ShapeDtypeStruct((r, width), given[0].dtype) for r in rows],
        scratch_shapes=[
            pltpu.VMEM((pixels, LANES), jnp.float32),
            pltpu.VMEM((max(rows), LANES), jnp.float32),
        ],
        compiler_params=PARAMS,
    )(*given)


def copy_all(copies):
    for copy in copies:
        copy.start()
    for copy in copies:
        copy.wait()


def build(x_ref, views, groups):
    width = x_ref.shape[1]
    strip = lax.broadcasted_iota(jnp.int32, (PIECE, width), 0) % STRIPS

    def put(at, block):
        at = pl.multiple_of(at, PIECE)
        none = jnp.zeros((EIGHT, width), jnp.float32)
        views[1, pl.ds(at, PIECE), :] = block.astype(jnp.bfloat16)
        before = jnp.concatenate([none, block[: PIECE - EIGHT]], axis=0)
        views[0, pl.ds(at, PIECE), :] = before.astype(jnp.bfloat16)
        after = jnp.concatenate([block[EIGHT:], none], axis=0)
        views[2, pl.ds(at, PIECE), :] = after.astype(jnp.bfloat16)

    def load(at):
        return x_ref[pl.ds(pl.multiple_of(at, PIECE), PIECE), :].astype(jnp.float32)

    def turn(block, by):
        return pltpu.roll(block.reshape(WW, EIGHT, width), by, 1).reshape(PIECE, width)

    @pl.loop(0, DEEP * groups)
    def _(n):
        put((groups + n) * PIECE, load(n * PIECE))

    @pl.loop(0, groups)
    def _(g):
        above = turn(load(((DEEP - 1) * groups + g) * PIECE), 1)
        put(g * PIECE, jnp.where(strip == 0, 0.0, above))
        below = turn(load(g * PIECE), EIGHT - 1)
        put(((DEEP + 1) * groups + g) * PIECE, jnp.where(strip == STRIPS - 1, 0.0, below))


def tap_rows(views, groups, row, col):
    start = row * (groups * PIECE)
    if not isinstance(row, int):
        start = pl.multiple_of(start, PIECE)
    return views[col, pl.ds(start, groups * GROUP), :]


def views_shape(groups, width):
    return pltpu.VMEM((3, (DEEP + 2) * groups * PIECE, width), jnp.bfloat16)


HALF, CHIP, PLACE, SHARDS = 0, 1, 2, 3


def tangent_kernel(groups, sources, slots, more, last, meta, *refs):
    count = len(slots)
    given = 1 + max(n for order in sources for n in order)
    shards = refs[:given]
    v_ref, w_ref = refs[given : given + 2]
    before = refs[given + 2] if more else None
    refs = refs[given + 2 + more :]
    if last:
        send_ref, keep_ref, xt_ref, x, xt, views, sem, *refs = refs
        acc, *refs = refs
    else:
        acc, xt_ref, x, xt, views, sem, *refs = refs
    away = pltpu.make_async_copy(xt, xt_ref, sem.at[count + 2])
    own = v_ref.shape[1] // len(sources)
    step = pl.program_id(0)

    @pl.when(step == 0)
    def _():
        fetch = []
        if count == 1:
            at = pl.ds(pl.multiple_of(meta[SHARDS + slots[0]] * own, own), own)
            for n, ref in enumerate((v_ref, w_ref)):
                to = refs[0].at[:, pl.ds(n * own, own), :]
                fetch.append(pltpu.make_async_copy(ref.at[:, at, :], to, sem.at[count + n]))
        for copy in fetch:
            copy.start()
        for z, order in enumerate(sources):

            @pl.when(meta[PLACE] == z)
            def _():
                copy_all(
                    [
                        pltpu.make_async_copy(
                            shards[n],
                            x.at[:, pl.ds(i * LANES, LANES)],
                            sem.at[i],
                        )
                        for i, n in enumerate(order)
                    ]
                )

        build(x, views, groups)
        for i in range(count):
            turned = x[:, i * LANES : (i + 1) * LANES].astype(jnp.float32).T
            xt[i * own : (i + 1) * own, :] = turned[:own].astype(jnp.bfloat16)
        away.start()
        for copy in fetch:
            copy.wait()

    if count == 1:
        lhs = [tap_rows(views, groups, row, col) for row in range(3) for col in range(3)]
        rhs = refs[0][...].reshape(9 * LANES, acc.shape[1])
    else:
        lhs, rhs = [], []
        for col in range(3):
            lhs.append(tap_rows(views, groups, step, col))
            for slot in slots:
                at = pl.ds(pl.multiple_of(meta[SHARDS + slot] * own, own), own)
                rhs += [v_ref[col, at, :], w_ref[col, at, :]]
        rhs = jnp.concatenate(rhs, axis=0)
    value = jnp.dot(jnp.concatenate(lhs, axis=1), rhs, preferred_element_type=jnp.float32)
    pl.when(step == pl.num_programs(0) - 1)(away.wait)
    if count == 1:
        acc[...] = before[...] + value if more else value
    elif more:
        acc[...] = value + jnp.where(step == 0, before[...], acc[...])
    else:
        acc[...] = jnp.where(step == 0, value, acc[...] + value)
    if last:
        pl.when(step == pl.num_programs(0) - 1)(
            functools.partial(halves, meta, acc, send_ref, keep_ref)
        )


def halves(meta, acc, send_ref, keep_ref):
    half, n = meta[HALF], acc.shape[0] // 2
    mine = pl.ds(pl.multiple_of(half * n, n), n)
    other = pl.ds(pl.multiple_of((1 - half) * n, n), n)
    send_ref[...] = acc[other, :].astype(jnp.bfloat16)
    keep_ref[...] = acc[mine, :]


def tangent(meta, shards, sources, slots, v, w, groups, before, last):
    more = before is not None
    rows = groups * GROUP
    channels, filters = w.shape[1:]
    count = len(slots)
    own = channels // len(sources)
    whole_block = pl.BlockSpec(memory_space=pl.ANY)
    row_block = pl.BlockSpec((3, channels, filters), lambda t, m: (t, 0, 0))

    def whole(*shape):
        return pl.BlockSpec(shape, lambda t, m: (0,) * len(shape))

    hbm = pl.BlockSpec(memory_space=pltpu.HBM)
    if last:
        out_specs = [whole(rows // 2, filters)] * 2
        outs = [
            jax.ShapeDtypeStruct((rows // 2, filters), jnp.bfloat16),
            jax.ShapeDtypeStruct((rows // 2, filters), jnp.float32),
        ]
    else:
        out_specs = [whole(rows, filters)]
        outs = [jax.ShapeDtypeStruct((rows, filters), jnp.float32)]
    return pl.pallas_call(
        functools.partial(tangent_kernel, groups, sources, slots, more, last),
        grid_spec=pltpu.PrefetchScalarGridSpec(
            num_scalar_prefetch=1,
            grid=(1 if count == 1 else 3,),
            in_specs=[whole_block] * len(shards)
            + [whole_block if count == 1 else row_block] * 2
            + ([whole(rows, filters)] if more else []),
            out_specs=out_specs + [hbm],
            scratch_shapes=[
                pltpu.VMEM((rows, count * LANES), jnp.bfloat16),
                pltpu.VMEM((count * own, rows), jnp.bfloat16),
                views_shape(groups, count * LANES),
                pltpu.SemaphoreType.DMA((count + 3,)),
            ]
            + ([pltpu.VMEM((rows, filters), jnp.float32)] if last else [])
            + ([pltpu.VMEM((9, LANES, filters), jnp.bfloat16)] if count == 1 else []),
        ),
        out_shape=outs + [pltpu.HBM((count * own, rows), jnp.bfloat16)],
        cost_estimate=pl.CostEstimate(
            flops=18 * rows * count * LANES * filters,
            bytes_accessed=4 * w.size,
            transcendentals=0,
        ),
        name="tangent",
        compiler_params=PARAMS,
    )(meta, *shards, v, w, *([before] if more else []))


def split_kernel(meta, keep_ref, got_ref, mine_ref, *parts):
    for m in range(1 + len(parts)):
        at = pl.multiple_of((meta[CHIP] ^ m) * LANES, LANES)
        total = keep_ref[:, pl.ds(at, LANES)] + got_ref[:, pl.ds(at, LANES)].astype(jnp.float32)
        if m:
            parts[m - 1][...] = total.astype(jnp.bfloat16)
        else:
            mine_ref[...] = total


def split(meta, keep, got):
    rows, filters = keep.shape
    block = pl.BlockSpec((rows, filters), lambda t, m: (0, 0))
    out = pl.BlockSpec((rows, LANES), lambda t, m: (0, 0))
    kinds = [jnp.float32] + [jnp.bfloat16] * (filters // LANES - 1)
    return pl.pallas_call(
        split_kernel,
        grid_spec=pltpu.PrefetchScalarGridSpec(
            num_scalar_prefetch=1, grid=(1,), in_specs=[block] * 2, out_specs=[out] * len(kinds)
        ),
        out_shape=[jax.ShapeDtypeStruct((rows, LANES), kind) for kind in kinds],
        cost_estimate=pl.CostEstimate(
            flops=rows * filters, bytes_accessed=8 * keep.size, transcendentals=0
        ),
        name="split",
        compiler_params=PARAMS,
    )(meta, keep, got)


def gather_parts(meta, parts, x, sem):
    blocks, rows = len(parts) // 2, x.shape[0] // 2
    copies = []
    for n, part in enumerate(parts):
        half = meta[HALF] if n < blocks else 1 - meta[HALF]
        at = pl.multiple_of(half * rows, rows)
        lane = pl.multiple_of((meta[CHIP] ^ (n % blocks)) * LANES, LANES)
        to = x.at[pl.ds(at, rows), pl.ds(lane, LANES)]
        copies.append(pltpu.make_async_copy(part, to, sem.at[n]))
    copy_all(copies)


def cotangent_kernel(groups, places, parts, meta, *refs):
    outs = refs[-6 - parts : -6]
    w_parts, k_ref = refs[: -7 - parts], refs[-7 - parts]
    rows_ref, x, views, sem, acc, flat = refs[-6:]
    step = pl.program_id(0)
    keep = pltpu.make_async_copy(x, rows_ref, sem.at[len(w_parts)])

    @pl.when(step == 0)
    def _():
        gather_parts(meta, w_parts, x, sem)
        keep.start()
        build(x, views, len(groups))

    value = lax.dot_general(
        jnp.concatenate(
            [tap_rows(views, len(groups), 2 - step, 2 - col) for col in range(3)], axis=1
        ),
        jnp.concatenate([k_ref[col] for col in range(3)], axis=1),
        (((1,), (1,)), ((), ())),
        preferred_element_type=jnp.float32,
    )
    for n in range(acc.shape[0]):
        column = value[:, n * LANES : (n + 1) * LANES]
        acc[n] = jnp.where(step == 0, column, acc[n] + column)

    @pl.when(step == 2)
    def _():
        keep.wait()
        for n in range(acc.shape[0]):
            for g, strip, deep, _, row in pieces_of(groups):
                target = places[g, strip] + deep * WW
                flat[pl.ds(target, WW), :] = acc[n, pl.ds(row, WW, stride=EIGHT), :]
            share = flat.shape[0] // parts
            for m, out in enumerate(outs):
                at = pl.multiple_of((meta[PLACE] ^ m) * share, share)
                cols = pl.ds(n * LANES, LANES)
                out[:, cols] = flat[pl.ds(at, share), :].astype(out.dtype)


def cotangent_part(meta, w_parts, groups, kernel, places, parts):
    channels, filters = kernel.shape[1:]
    rows = 2 * w_parts[0].shape[0]
    return pl.pallas_call(
        functools.partial(cotangent_kernel, groups, places, parts),
        grid_spec=pltpu.PrefetchScalarGridSpec(
            num_scalar_prefetch=1,
            grid=(3,),
            in_specs=[pl.BlockSpec(memory_space=pl.ANY)] * len(w_parts)
            + [pl.BlockSpec((3, channels, filters), lambda t, m: (t, 0, 0))],
            out_specs=[pl.BlockSpec((rows // parts, channels), lambda t, m: (0, 0))] * parts
            + [pl.BlockSpec(memory_space=pltpu.HBM)],
            scratch_shapes=[
                pltpu.VMEM((rows, filters), jnp.bfloat16),
                views_shape(len(groups), filters),
                pltpu.SemaphoreType.DMA((len(w_parts) + 1,)),
                pltpu.VMEM((channels // LANES, rows, LANES), jnp.float32),
                pltpu.VMEM((rows, LANES), jnp.float32),
            ],
        ),
        out_shape=[
            jax.ShapeDtypeStruct((rows // parts, channels), jnp.bfloat16 if m else jnp.float32)
            for m in range(parts)
        ]
        + [pltpu.HBM((rows, filters), jnp.bfloat16)],
        cost_estimate=pl.CostEstimate(
            flops=18 * rows * channels * filters,
            bytes_accessed=18 * channels * filters,
            transcendentals=0,
        ),
        name="cotangent",
        compiler_params=PARAMS,
    )(meta, *w_parts, kernel)


def product_kernel(own, counts, sizes, scale, meta, *refs):
    chunks = len(counts)
    scratch = refs[-2 * chunks :]
    given, out_ref = refs[: -1 - 2 * chunks], refs[-1 - 2 * chunks]
    ends = [sum(sizes[: n + 1]) for n in range(chunks)]
    tap = pl.program_id(0)

    @pl.when(tap == 0)
    def _():
        for n, count in enumerate(counts):
            w_ref, *xts = given[ends[n] - sizes[n] : ends[n]]
            views, xt = scratch[2 * n : 2 * n + 2]
            build(w_ref, views, count)
            slot = 0
            for ref in xts:
                for row in range(0, ref.shape[0], own):
                    at = pl.multiple_of(meta[SHARDS + slot] * own, own)
                    xt[pl.ds(at, own), :] = ref[pl.ds(row, own), :]
                    slot += 1

    value = None
    for n, count in enumerate(counts):
        views, xt = scratch[2 * n : 2 * n + 2]
        term = jnp.dot(
            xt[...], tap_rows(views, count, 2 - tap // 3, 2 - lax.rem(tap, 3)), preferred_element_type=jnp.float32
        )
        value = term if value is None else value + term
    out_ref[0] = value * scale


def product_of(meta, chunks, counts, scale, channels, own):
    given = [array for chunk in chunks for array in chunk]
    total = sum(chunk[0].shape[0] for chunk in chunks)
    filters = chunks[0][0].shape[1]
    scratch = []
    for (w, *_), count in zip(chunks, counts):
        scratch += [views_shape(count, filters), pltpu.VMEM((channels, w.shape[0]), jnp.bfloat16)]
    return pl.pallas_call(
        functools.partial(product_kernel, own, counts, [len(chunk) for chunk in chunks], scale),
        grid_spec=pltpu.PrefetchScalarGridSpec(
            num_scalar_prefetch=1,
            grid=(9,),
            in_specs=[pl.BlockSpec(array.shape, lambda t, m: (0, 0)) for array in given],
            out_specs=pl.BlockSpec((1, channels, filters), lambda t, m: (t, 0, 0)),
            scratch_shapes=scratch,
        ),
        out_shape=jax.ShapeDtypeStruct((9, channels, filters), jnp.float32),
        cost_estimate=pl.CostEstimate(
            flops=18 * total * channels * filters,
            bytes_accessed=36 * channels * filters,
            transcendentals=0,
        ),
        name="product",
        compiler_params=PARAMS,
    )(meta, *given)


def pack_kernel(s_ref, c_ref, out_ref):
    rows = s_ref.shape[0]
    each = out_ref.shape[1] // 2
    for n in range(out_ref.shape[0]):
        cols = pl.ds(n // 2 * LANES, LANES)
        for kind, ref in enumerate((s_ref, c_ref)):
            out_ref[n, kind * each : kind * each + rows, :] = ref[:, cols]
            rest = jnp.zeros((each - rows, LANES), out_ref.dtype)
            out_ref[n, kind * each + rows : (kind + 1) * each, :] = rest


def pack(slope, curvature):
    rows, filters = slope.shape
    each = -(-rows // 16) * 16
    return pl.pallas_call(
        pack_kernel,
        out_shape=jax.ShapeDtypeStruct((2 * filters // LANES, 2 * each, LANES), slope.dtype),
        name="pack",
        compiler_params=PARAMS,
    )(slope, curvature)


def block_program(activations, act_tangent, kernel, kernel_tangent, slope, curvature):
    z, me = lax.axis_index("filt"), lax.axis_index("chan")
    depth, across = lax.axis_size("filt"), lax.axis_size("chan")
    half, chips = lax.rem(me, 2), across // 2
    pixels, own = activations.shape
    channels = kernel.shape[1]

    per = 2 * (pixels // (HH * WW)) // depth
    outer, inner = [], []
    for image in range(per * depth // 2):
        (inner if abs(image % per - per // 2) <= INNER else outer).append(image)
    chunks = [list(zip(images[::PAIR], images[1::PAIR])) for images in (outer, inner)]

    orders, owners = [], []
    for place in range(depth):
        order, owner = [(0, 0)], [place]
        for step in range(1, depth):
            for link in range(2):
                shard = place + step if place % 2 == link else place - step
                if 0 <= shard < depth:
                    order.append((step, link))
                    owner.append(shard)
        orders.append(order)
        owners.append(owner)
    table = [
        [n % 2, n // 2, place] + owners[place]
        for place in range(depth)
        for n in range(across)
    ]
    meta = lax.dynamic_index_in_dim(
        jnp.asarray(table, jnp.int32), z * across + me, 0, keepdims=False
    )

    mixed = sort_call(mix_kernel, chunks, [activations.T, act_tangent.T], pixels, 2 * own)

    packed = pack(slope, curvature)
    packed = lax.all_to_all(packed, "chan", 0, 0, tiled=True)
    factors = sort_call(sort_kernel, chunks, [packed], pixels, 2 * LANES)

    def gathered(x):
        got = {(0, 0): x}
        last = [x, x]
        for step in range(1, depth):
            now = [None, None]
            for link in range(2):
                pairs = []
                for i in range(link, depth - 1, 2):
                    pairs += [(i, i + 1)] * (i >= step - 1) + [(i + 1, i)] * (i + 1 <= depth - step)
                if pairs:
                    now[link] = lax.ppermute(last[1 - link], "filt", pairs)
                    got[step, link] = now[link]
            last = now
        return got

    def swap(x, bit):
        return lax.ppermute(x, "chan", [(i, i ^ bit) for i in range(across)])

    def some(slots, c):
        names = sorted({order[slot] for order in orders for slot in slots})
        sources = [[names.index(order[slot]) for slot in slots] for order in orders]
        return [got[c][name] for name in names], sources

    def tangents(c):
        stages = [[0, 1], [2], [3]] if c == 0 else [[0, 1], [2, 3]]
        before, xts = None, []
        for n, slots in enumerate(stages):
            shards, sources = some(slots, c)
            *sums, xt = tangent(
                meta,
                shards,
                sources,
                slots,
                pltpu.with_memory_space_constraint(kernel_tangent, pltpu.HBM),
                pltpu.with_memory_space_constraint(kernel, pltpu.HBM),
                len(chunks[c]),
                before,
                n == len(stages) - 1,
            )
            before = sums[0]
            xts.append(xt)
        return sums, xts

    def exchange(send, keep):
        got = swap(send, 1)
        mine, *parts = split(meta, keep, got)
        for m, part in enumerate(parts):
            mine = mine + swap(part, 2 * (m + 1)).astype(jnp.float32)
        return mine

    def weighted(mine, factor):
        rows = mine.shape[0]
        factor = lax.dynamic_slice_in_dim(factor, half * rows, rows, axis=0)
        w = weigh(factor[:, :LANES], factor[:, LANES:], mine)
        parts = [w] + [swap(w, 2 * m) for m in range(1, chips)]
        parts += [swap(part, 1) for part in parts]
        return [pltpu.with_memory_space_constraint(part, pltpu.HBM) for part in parts]

    def places_of(groups):
        strip_rows = GROUP // EIGHT
        sources = {}
        for g, images in enumerate(groups):
            for strip in range(EIGHT):
                row = images[strip // STRIPS] * HH * WW + strip % STRIPS * strip_rows
                sources[row] = (g, strip)
        return {sources[row]: n * strip_rows for n, row in enumerate(sorted(sources))}

    def spread(own_part, parts):
        total = own_part
        for m, part in enumerate(parts):
            part = lax.ppermute(part, "filt", [(i, i ^ (m + 1)) for i in range(depth)])
            total = total + part.astype(jnp.float32)
        return total.astype(jnp.bfloat16)

    got = [gathered(x) for x in mixed]
    sums, xts = zip(*[tangents(c) for c in range(2)])
    mine = [exchange(*sums[c]) for c in range(2)]
    w = [weighted(mine[c], factors[c]) for c in range(2)]
    cots, whole = [], []
    kernel_hbm = pltpu.with_memory_space_constraint(kernel, pltpu.HBM)
    for c, place in enumerate([places_of(groups) for groups in chunks]):
        own_part, *parts, rows = cotangent_part(meta, w[c], chunks[c], kernel_hbm, place, depth)
        cots.append(spread(own_part, parts))
        whole.append(rows)
    scale = float(1.0 / (float(pixels) ** 0.5))
    product = product_of(
        meta,
        [(whole[c], *xts[c]) for c in range(2)],
        [len(groups) for groups in chunks],
        scale,
        channels,
        own,
    )
    result = jnp.where(
        lax.rem(z, 2) == 0, jnp.concatenate(cots, axis=0), jnp.concatenate(cots[::-1], axis=0)
    )
    return (result, product)


def block_device(*args):
    return block_program(*args)


def fits(mesh, pixels, channels, filters):
    depth, across = mesh.shape["filt"], mesh.shape["chan"]
    images = pixels // (HH * WW)
    return (
        depth == 2 * PAIR
        and 2 * images == 9 * depth
        and across == 8
        and 2 * channels == LANES * across * depth
        and filters == LANES * (across // 2) * depth
    )


def solution(mesh):
    in_specs = (
        P(None, ("chan", "filt")),
        P(None, ("chan", "filt")),
        P(None, "chan", "filt"),
        P(None, "chan", "filt"),
        P("chan", "filt"),
        P("chan", "filt"),
    )

    def program(*args):
        pixels, channels = args[0].shape
        body = block_device if fits(mesh, pixels, channels, args[2].shape[2]) else any_device
        return jax.shard_map(
            body,
            mesh=mesh,
            in_specs=in_specs,
            out_specs=(P("filt", "chan"), P(None, "chan", "filt")),
            check_vma=False,
        )(*args)

    return program
```

```python
import functools

import jax
import jax.numpy as jnp
from jax import lax
from jax.experimental import pallas as pl
from jax.experimental.pallas import tpu as pltpu
from jax.sharding import PartitionSpec as P


HH = 12
WW = 12
LANES = 128
STRIPS = 4
DEEP = HH // STRIPS
PAIR = 2
EIGHT = PAIR * STRIPS
PIECE = WW * EIGHT
GROUP = DEEP * PIECE

INNER = 1
PARAMS = pltpu.CompilerParams(vmem_limit_bytes=28 << 20)


def windows(flat, flip):
    width = flat.shape[-1]
    image = flat.reshape(-1, HH, WW, width)
    padded = jnp.pad(image, ((0, 0), (1, 1), (1, 1), (0, 0)))
    result = []
    for row_tap in range(3):
        for col_tap in range(3):
            top = 2 - row_tap if flip else row_tap
            left = 2 - col_tap if flip else col_tap
            result.append(padded[:, top : top + HH, left : left + WW, :].reshape(-1, width))
    return result


def weigh(slope, curvature, tangent):
    slope_f = slope.astype(jnp.float32)
    return (slope_f * slope_f * curvature.astype(jnp.float32) * tangent).astype(jnp.bfloat16)


def any_device(activations, act_tangent, kernel, kernel_tangent, slope, curvature):
    acts_block, tans_block = (
        lax.all_gather(activations, "filt", axis=1, tiled=True),
        lax.all_gather(act_tangent, "filt", axis=1, tiled=True),
    )
    acts = windows(acts_block, False)
    tans = windows(tans_block, False)
    pixel_count = acts_block.shape[0]
    partial_value = jnp.zeros((pixel_count, kernel.shape[2]), jnp.float32)
    for tap in range(9):
        partial_value = partial_value + jnp.dot(
            tans[tap], kernel[tap], preferred_element_type=jnp.float32
        )
        partial_value = partial_value + jnp.dot(
            acts[tap], kernel_tangent[tap], preferred_element_type=jnp.float32
        )
    total = lax.psum(partial_value, "chan")
    slope_all, curve_all = (
        lax.all_gather(slope, "chan", axis=0, tiled=True),
        lax.all_gather(curvature, "chan", axis=0, tiled=True),
    )
    weighted = weigh(slope_all, curve_all, total)
    backs = windows(weighted, True)
    cot_part = jnp.zeros((pixel_count, kernel.shape[1]), jnp.float32)
    grads = []
    for tap in range(9):
        cot_part = cot_part + lax.dot_general(
            backs[tap], kernel[tap], (((1,), (1,)), ((), ())), preferred_element_type=jnp.float32
        )
        grads.append(
            lax.dot_general(
                acts[tap], weighted, (((0,), (0,)), ((), ())), preferred_element_type=jnp.float32
            )
        )
    kernel_product = jnp.stack(grads) / jnp.sqrt(jnp.float32(pixel_count))
    cotangent = lax.psum_scatter(cot_part, "filt", scatter_dimension=0, tiled=True).astype(
        jnp.bfloat16
    )
    return (cotangent, kernel_product)


def pieces_of(groups):
    for g, images in enumerate(groups):
        for strip in range(EIGHT):
            image, part = images[strip // STRIPS], strip % STRIPS
            for deep in range(DEEP):
                source = (image * HH + part * DEEP + deep) * WW
                yield g, strip, deep, source, (deep * len(groups) + g) * PIECE + strip


def sort_into(chunks, flat, sorted_, outs, cols):
    for groups, out in zip(chunks, outs):
        for _, _, _, source, target in pieces_of(groups):
            sorted_[pl.ds(target, WW, stride=EIGHT), :] = flat[pl.ds(source, WW), :]
        out[:, cols] = sorted_[pl.ds(0, out.shape[0]), :].astype(out.dtype)


def sort_kernel(chunks, x_ref, *refs):
    outs, (flat, sorted_) = refs[: len(chunks)], refs[len(chunks) :]
    blocks, each = x_ref.shape[0], x_ref.shape[1] // 2
    rows = flat.shape[0] // blocks
    for kind in range(2):
        for n in range(blocks):
            block = x_ref[n, kind * each : (kind + 1) * each, :].astype(jnp.float32)
            flat[n * rows : (n + 1) * rows, :] = block[:rows]
        sort_into(chunks, flat, sorted_, outs, pl.ds(kind * LANES, LANES))


def mix_kernel(chunks, a_ref, t_ref, *refs):
    outs, (flat, sorted_) = refs[: len(chunks)], refs[len(chunks) :]
    both = jnp.concatenate(
        [a_ref[...].astype(jnp.float32), t_ref[...].astype(jnp.float32)], axis=0
    )
    flat[...] = both.T
    sort_into(chunks, flat, sorted_, outs, pl.ds(0, LANES))


def sort_call(kernel, chunks, given, pixels, width):
    rows = [len(groups) * GROUP for groups in chunks]
    return pl.pallas_call(
        functools.partial(kernel, chunks),
        out_shape=[jax.ShapeDtypeStruct((r, width), given[0].dtype) for r in rows],
        scratch_shapes=[
            pltpu.VMEM((pixels, LANES), jnp.float32),
            pltpu.VMEM((max(rows), LANES), jnp.float32),
        ],
        compiler_params=PARAMS,
    )(*given)


def copy_all(copies):
    for copy in copies:
        copy.start()
    for copy in copies:
        copy.wait()


def build(x_ref, views, groups):
    width = x_ref.shape[1]
    strip = lax.broadcasted_iota(jnp.int32, (PIECE, width), 0) % STRIPS

    def put(at, block):
        at = pl.multiple_of(at, PIECE)
        none = jnp.zeros((EIGHT, width), jnp.float32)
        views[1, pl.ds(at, PIECE), :] = block.astype(jnp.bfloat16)
        before = jnp.concatenate([none, block[: PIECE - EIGHT]], axis=0)
        views[0, pl.ds(at, PIECE), :] = before.astype(jnp.bfloat16)
        after = jnp.concatenate([block[EIGHT:], none], axis=0)
        views[2, pl.ds(at, PIECE), :] = after.astype(jnp.bfloat16)

    def load(at):
        return x_ref[pl.ds(pl.multiple_of(at, PIECE), PIECE), :].astype(jnp.float32)

    def turn(block, by):
        return pltpu.roll(block.reshape(WW, EIGHT, width), by, 1).reshape(PIECE, width)

    @pl.loop(0, DEEP * groups)
    def _(n):
        put((groups + n) * PIECE, load(n * PIECE))

    @pl.loop(0, groups)
    def _(g):
        above = turn(load(((DEEP - 1) * groups + g) * PIECE), 1)
        put(g * PIECE, jnp.where(strip == 0, 0.0, above))
        below = turn(load(g * PIECE), EIGHT - 1)
        put(((DEEP + 1) * groups + g) * PIECE, jnp.where(strip == STRIPS - 1, 0.0, below))


def tap_rows(views, groups, row, col):
    start = row * (groups * PIECE)
    if not isinstance(row, int):
        start = pl.multiple_of(start, PIECE)
    return views[col, pl.ds(start, groups * GROUP), :]


def views_shape(groups, width):
    return pltpu.VMEM((3, (DEEP + 2) * groups * PIECE, width), jnp.bfloat16)


HALF, CHIP, PLACE, SHARDS = 0, 1, 2, 3


def tangent_kernel(groups, sources, slots, more, last, meta, *refs):
    count = len(slots)
    given = 1 + max(n for order in sources for n in order)
    shards = refs[:given]
    v_ref, w_ref = refs[given : given + 2]
    before = refs[given + 2] if more else None
    refs = refs[given + 2 + more :]
    if last:
        send_ref, keep_ref, xt_ref, x, xt, views, sem, *refs = refs
        acc, *refs = refs
    else:
        acc, xt_ref, x, xt, views, sem, *refs = refs
    away = pltpu.make_async_copy(xt, xt_ref, sem.at[count + 2])
    own = v_ref.shape[1] // len(sources)
    step = pl.program_id(0)

    @pl.when(step == 0)
    def _():
        fetch = []
        if count == 1:
            at = pl.ds(pl.multiple_of(meta[SHARDS + slots[0]] * own, own), own)
            for n, ref in enumerate((v_ref, w_ref)):
                to = refs[0].at[:, pl.ds(n * own, own), :]
                fetch.append(pltpu.make_async_copy(ref.at[:, at, :], to, sem.at[count + n]))
        for copy in fetch:
            copy.start()
        for z, order in enumerate(sources):

            @pl.when(meta[PLACE] == z)
            def _():
                copy_all(
                    [
                        pltpu.make_async_copy(
                            shards[n],
                            x.at[:, pl.ds(i * LANES, LANES)],
                            sem.at[i],
                        )
                        for i, n in enumerate(order)
                    ]
                )

        build(x, views, groups)
        for i in range(count):
            turned = x[:, i * LANES : (i + 1) * LANES].astype(jnp.float32).T
            xt[i * own : (i + 1) * own, :] = turned[:own].astype(jnp.bfloat16)
        away.start()
        for copy in fetch:
            copy.wait()

    if count == 1:
        lhs = [tap_rows(views, groups, row, col) for row in range(3) for col in range(3)]
        rhs = refs[0][...].reshape(9 * LANES, acc.shape[1])
    else:
        lhs, rhs = [], []
        for col in range(3):
            lhs.append(tap_rows(views, groups, step, col))
            for slot in slots:
                at = pl.ds(pl.multiple_of(meta[SHARDS + slot] * own, own), own)
                rhs += [v_ref[col, at, :], w_ref[col, at, :]]
        rhs = jnp.concatenate(rhs, axis=0)
    value = jnp.dot(jnp.concatenate(lhs, axis=1), rhs, preferred_element_type=jnp.float32)
    pl.when(step == pl.num_programs(0) - 1)(away.wait)
    if count == 1:
        acc[...] = before[...] + value if more else value
    elif more:
        acc[...] = value + jnp.where(step == 0, before[...], acc[...])
    else:
        acc[...] = jnp.where(step == 0, value, acc[...] + value)
    if last:
        pl.when(step == pl.num_programs(0) - 1)(
            functools.partial(halves, meta, acc, send_ref, keep_ref)
        )


def halves(meta, acc, send_ref, keep_ref):
    half, n = meta[HALF], acc.shape[0] // 2
    mine = pl.ds(pl.multiple_of(half * n, n), n)
    other = pl.ds(pl.multiple_of((1 - half) * n, n), n)
    send_ref[...] = acc[other, :].astype(jnp.bfloat16)
    keep_ref[...] = acc[mine, :]


def tangent(meta, shards, sources, slots, v, w, groups, before, last):
    more = before is not None
    rows = groups * GROUP
    channels, filters = w.shape[1:]
    count = len(slots)
    own = channels // len(sources)
    whole_block = pl.BlockSpec(memory_space=pl.ANY)
    row_block = pl.BlockSpec((3, channels, filters), lambda t, m: (t, 0, 0))

    def whole(*shape):
        return pl.BlockSpec(shape, lambda t, m: (0,) * len(shape))

    hbm = pl.BlockSpec(memory_space=pltpu.HBM)
    if last:
        out_specs = [whole(rows // 2, filters)] * 2
        outs = [
            jax.ShapeDtypeStruct((rows // 2, filters), jnp.bfloat16),
            jax.ShapeDtypeStruct((rows // 2, filters), jnp.float32),
        ]
    else:
        out_specs = [whole(rows, filters)]
        outs = [jax.ShapeDtypeStruct((rows, filters), jnp.float32)]
    return pl.pallas_call(
        functools.partial(tangent_kernel, groups, sources, slots, more, last),
        grid_spec=pltpu.PrefetchScalarGridSpec(
            num_scalar_prefetch=1,
            grid=(1 if count == 1 else 3,),
            in_specs=[whole_block] * len(shards)
            + [whole_block if count == 1 else row_block] * 2
            + ([whole(rows, filters)] if more else []),
            out_specs=out_specs + [hbm],
            scratch_shapes=[
                pltpu.VMEM((rows, count * LANES), jnp.bfloat16),
                pltpu.VMEM((count * own, rows), jnp.bfloat16),
                views_shape(groups, count * LANES),
                pltpu.SemaphoreType.DMA((count + 3,)),
            ]
            + ([pltpu.VMEM((rows, filters), jnp.float32)] if last else [])
            + ([pltpu.VMEM((9, LANES, filters), jnp.bfloat16)] if count == 1 else []),
        ),
        out_shape=outs + [pltpu.HBM((count * own, rows), jnp.bfloat16)],
        cost_estimate=pl.CostEstimate(
            flops=18 * rows * count * LANES * filters,
            bytes_accessed=4 * w.size,
            transcendentals=0,
        ),
        name="tangent",
        compiler_params=PARAMS,
    )(meta, *shards, v, w, *([before] if more else []))


def split_kernel(meta, keep_ref, got_ref, mine_ref, *parts):
    for m in range(1 + len(parts)):
        at = pl.multiple_of((meta[CHIP] ^ m) * LANES, LANES)
        total = keep_ref[:, pl.ds(at, LANES)] + got_ref[:, pl.ds(at, LANES)].astype(jnp.float32)
        if m:
            parts[m - 1][...] = total.astype(jnp.bfloat16)
        else:
            mine_ref[...] = total


def split(meta, keep, got):
    rows, filters = keep.shape
    block = pl.BlockSpec((rows, filters), lambda t, m: (0, 0))
    out = pl.BlockSpec((rows, LANES), lambda t, m: (0, 0))
    kinds = [jnp.float32] + [jnp.bfloat16] * (filters // LANES - 1)
    return pl.pallas_call(
        split_kernel,
        grid_spec=pltpu.PrefetchScalarGridSpec(
            num_scalar_prefetch=1, grid=(1,), in_specs=[block] * 2, out_specs=[out] * len(kinds)
        ),
        out_shape=[jax.ShapeDtypeStruct((rows, LANES), kind) for kind in kinds],
        cost_estimate=pl.CostEstimate(
            flops=rows * filters, bytes_accessed=8 * keep.size, transcendentals=0
        ),
        name="split",
        compiler_params=PARAMS,
    )(meta, keep, got)


def gather_parts(meta, parts, x, sem):
    blocks, rows = len(parts) // 2, x.shape[0] // 2
    copies = []
    for n, part in enumerate(parts):
        half = meta[HALF] if n < blocks else 1 - meta[HALF]
        at = pl.multiple_of(half * rows, rows)
        lane = pl.multiple_of((meta[CHIP] ^ (n % blocks)) * LANES, LANES)
        to = x.at[pl.ds(at, rows), pl.ds(lane, LANES)]
        copies.append(pltpu.make_async_copy(part, to, sem.at[n]))
    copy_all(copies)


def cotangent_kernel(groups, places, parts, meta, *refs):
    outs = refs[-6 - parts : -6]
    w_parts, k_ref = refs[: -7 - parts], refs[-7 - parts]
    rows_ref, x, views, sem, acc, flat = refs[-6:]
    step = pl.program_id(0)
    keep = pltpu.make_async_copy(x, rows_ref, sem.at[len(w_parts)])

    @pl.when(step == 0)
    def _():
        gather_parts(meta, w_parts, x, sem)
        keep.start()
        build(x, views, len(groups))

    value = lax.dot_general(
        jnp.concatenate(
            [tap_rows(views, len(groups), 2 - step, 2 - col) for col in range(3)], axis=1
        ),
        jnp.concatenate([k_ref[col] for col in range(3)], axis=1),
        (((1,), (1,)), ((), ())),
        preferred_element_type=jnp.float32,
    )
    for n in range(acc.shape[0]):
        column = value[:, n * LANES : (n + 1) * LANES]
        acc[n] = jnp.where(step == 0, column, acc[n] + column)

    @pl.when(step == 2)
    def _():
        keep.wait()
        for n in range(acc.shape[0]):
            for g, strip, deep, _, row in pieces_of(groups):
                target = places[g, strip] + deep * WW
                flat[pl.ds(target, WW), :] = acc[n, pl.ds(row, WW, stride=EIGHT), :]
            share = flat.shape[0] // parts
            for m, out in enumerate(outs):
                at = pl.multiple_of((meta[PLACE] ^ m) * share, share)
                cols = pl.ds(n * LANES, LANES)
                out[:, cols] = flat[pl.ds(at, share), :].astype(out.dtype)


def cotangent_part(meta, w_parts, groups, kernel, places, parts, rows_space):
    channels, filters = kernel.shape[1:]
    rows = 2 * w_parts[0].shape[0]
    return pl.pallas_call(
        functools.partial(cotangent_kernel, groups, places, parts),
        grid_spec=pltpu.PrefetchScalarGridSpec(
            num_scalar_prefetch=1,
            grid=(3,),
            in_specs=[pl.BlockSpec(memory_space=pl.ANY)] * len(w_parts)
            + [pl.BlockSpec((3, channels, filters), lambda t, m: (t, 0, 0))],
            out_specs=[pl.BlockSpec((rows // parts, channels), lambda t, m: (0, 0))] * parts
            + [pl.BlockSpec(memory_space=rows_space)],
            scratch_shapes=[
                pltpu.VMEM((rows, filters), jnp.bfloat16),
                views_shape(len(groups), filters),
                pltpu.SemaphoreType.DMA((len(w_parts) + 1,)),
                pltpu.VMEM((channels // LANES, rows, LANES), jnp.float32),
                pltpu.VMEM((rows, LANES), jnp.float32),
            ],
        ),
        out_shape=[
            jax.ShapeDtypeStruct((rows // parts, channels), jnp.bfloat16 if m else jnp.float32)
            for m in range(parts)
        ]
        + [rows_space((rows, filters), jnp.bfloat16)],
        cost_estimate=pl.CostEstimate(
            flops=18 * rows * channels * filters,
            bytes_accessed=18 * channels * filters,
            transcendentals=0,
        ),
        name="cotangent",
        compiler_params=PARAMS,
    )(meta, *w_parts, kernel)


def product_kernel(own, counts, sizes, scale, meta, *refs):
    chunks = len(counts)
    scratch = refs[-2 * chunks :]
    given, out_ref = refs[: -1 - 2 * chunks], refs[-1 - 2 * chunks]
    ends = [sum(sizes[: n + 1]) for n in range(chunks)]
    tap = pl.program_id(0)

    @pl.when(tap == 0)
    def _():
        for n, count in enumerate(counts):
            w_ref, *xts = given[ends[n] - sizes[n] : ends[n]]
            views, xt = scratch[2 * n : 2 * n + 2]
            build(w_ref, views, count)
            slot = 0
            for ref in xts:
                for row in range(0, ref.shape[0], own):
                    at = pl.multiple_of(meta[SHARDS + slot] * own, own)
                    xt[pl.ds(at, own), :] = ref[pl.ds(row, own), :]
                    slot += 1

    value = None
    for n, count in enumerate(counts):
        views, xt = scratch[2 * n : 2 * n + 2]
        term = jnp.dot(
            xt[...], tap_rows(views, count, 2 - tap // 3, 2 - lax.rem(tap, 3)), preferred_element_type=jnp.float32
        )
        value = term if value is None else value + term
    out_ref[0] = value * scale


def product_of(meta, chunks, counts, scale, channels, own):
    given = [array for chunk in chunks for array in chunk]
    total = sum(chunk[0].shape[0] for chunk in chunks)
    filters = chunks[0][0].shape[1]
    scratch = []
    for (w, *_), count in zip(chunks, counts):
        scratch += [views_shape(count, filters), pltpu.VMEM((channels, w.shape[0]), jnp.bfloat16)]
    return pl.pallas_call(
        functools.partial(product_kernel, own, counts, [len(chunk) for chunk in chunks], scale),
        grid_spec=pltpu.PrefetchScalarGridSpec(
            num_scalar_prefetch=1,
            grid=(9,),
            in_specs=[pl.BlockSpec(array.shape, lambda t, m: (0, 0)) for array in given],
            out_specs=pl.BlockSpec((1, channels, filters), lambda t, m: (t, 0, 0)),
            scratch_shapes=scratch,
        ),
        out_shape=jax.ShapeDtypeStruct((9, channels, filters), jnp.float32),
        cost_estimate=pl.CostEstimate(
            flops=18 * total * channels * filters,
            bytes_accessed=36 * channels * filters,
            transcendentals=0,
        ),
        name="product",
        compiler_params=PARAMS,
    )(meta, *given)


def pack_kernel(s_ref, c_ref, out_ref):
    rows = s_ref.shape[0]
    each = out_ref.shape[1] // 2
    for n in range(out_ref.shape[0]):
        cols = pl.ds(n // 2 * LANES, LANES)
        for kind, ref in enumerate((s_ref, c_ref)):
            out_ref[n, kind * each : kind * each + rows, :] = ref[:, cols]
            rest = jnp.zeros((each - rows, LANES), out_ref.dtype)
            out_ref[n, kind * each + rows : (kind + 1) * each, :] = rest


def pack(slope, curvature):
    rows, filters = slope.shape
    each = -(-rows // 16) * 16
    return pl.pallas_call(
        pack_kernel,
        out_shape=jax.ShapeDtypeStruct((2 * filters // LANES, 2 * each, LANES), slope.dtype),
        name="pack",
        compiler_params=PARAMS,
    )(slope, curvature)


def block_program(activations, act_tangent, kernel, kernel_tangent, slope, curvature):
    z, me = lax.axis_index("filt"), lax.axis_index("chan")
    depth, across = lax.axis_size("filt"), lax.axis_size("chan")
    half, chips = lax.rem(me, 2), across // 2
    pixels, own = activations.shape
    channels = kernel.shape[1]

    per = 2 * (pixels // (HH * WW)) // depth
    outer, inner = [], []
    for image in range(per * depth // 2):
        (inner if abs(image % per - per // 2) <= INNER else outer).append(image)
    chunks = [list(zip(images[::PAIR], images[1::PAIR])) for images in (outer, inner)]

    orders, owners = [], []
    for place in range(depth):
        order, owner = [(0, 0)], [place]
        for step in range(1, depth):
            for link in range(2):
                shard = place + step if place % 2 == link else place - step
                if 0 <= shard < depth:
                    order.append((step, link))
                    owner.append(shard)
        orders.append(order)
        owners.append(owner)
    table = [
        [n % 2, n // 2, place] + owners[place]
        for place in range(depth)
        for n in range(across)
    ]
    meta = lax.dynamic_index_in_dim(
        jnp.asarray(table, jnp.int32), z * across + me, 0, keepdims=False
    )

    mixed = sort_call(
        mix_kernel,
        chunks,
        [pltpu.with_memory_space_constraint(x.T, pltpu.HBM) for x in (activations, act_tangent)],
        pixels,
        2 * own,
    )

    packed = pack(slope, curvature)
    packed = lax.all_to_all(packed, "chan", 0, 0, tiled=True)
    factors = sort_call(sort_kernel, chunks, [packed], pixels, 2 * LANES)

    def gathered(x):
        got = {(0, 0): x}
        last = [x, x]
        for step in range(1, depth):
            now = [None, None]
            for link in range(2):
                pairs = []
                for i in range(link, depth - 1, 2):
                    pairs += [(i, i + 1)] * (i >= step - 1) + [(i + 1, i)] * (i + 1 <= depth - step)
                if pairs:
                    now[link] = lax.ppermute(last[1 - link], "filt", pairs)
                    got[step, link] = now[link]
            last = now
        return got

    def swap(x, bit):
        return lax.ppermute(x, "chan", [(i, i ^ bit) for i in range(across)])

    def some(slots, c):
        names = sorted({order[slot] for order in orders for slot in slots})
        sources = [[names.index(order[slot]) for slot in slots] for order in orders]
        return [got[c][name] for name in names], sources

    def tangents(c):
        stages = [[0, 1], [2], [3]] if c == 0 else [[0, 1], [2, 3]]
        before, xts = None, []
        for n, slots in enumerate(stages):
            shards, sources = some(slots, c)
            *sums, xt = tangent(
                meta,
                shards,
                sources,
                slots,
                pltpu.with_memory_space_constraint(kernel_tangent, pltpu.HBM),
                pltpu.with_memory_space_constraint(kernel, pltpu.HBM),
                len(chunks[c]),
                before,
                n == len(stages) - 1,
            )
            before = sums[0]
            xts.append(xt)
        return sums, xts

    def exchange(send, keep):
        got = swap(send, 1)
        mine, *parts = split(meta, keep, got)
        for m, part in enumerate(parts):
            mine = mine + swap(part, 2 * (m + 1)).astype(jnp.float32)
        return mine

    def weighted(mine, factor, c):
        rows = mine.shape[0]
        factor = lax.dynamic_slice_in_dim(factor, half * rows, rows, axis=0)
        w = weigh(factor[:, :LANES], factor[:, LANES:], mine)
        parts = [w] + [swap(w, 2 * m) for m in range(1, chips)]
        parts += [swap(part, 1) for part in parts]
        if c == 0:
            parts = [pltpu.with_memory_space_constraint(part, pltpu.HBM) for part in parts]
        return parts

    def places_of(groups):
        strip_rows = GROUP // EIGHT
        sources = {}
        for g, images in enumerate(groups):
            for strip in range(EIGHT):
                row = images[strip // STRIPS] * HH * WW + strip % STRIPS * strip_rows
                sources[row] = (g, strip)
        return {sources[row]: n * strip_rows for n, row in enumerate(sorted(sources))}

    def spread(own_part, parts):
        total = own_part
        for m, part in enumerate(parts):
            part = lax.ppermute(part, "filt", [(i, i ^ (m + 1)) for i in range(depth)])
            total = total + part.astype(jnp.float32)
        return total.astype(jnp.bfloat16)

    got = [gathered(x) for x in mixed]
    sums, xts = zip(*[tangents(c) for c in range(2)])
    mine = [exchange(*sums[c]) for c in range(2)]
    w = [weighted(mine[c], factors[c], c) for c in range(2)]
    cots, whole = [], []
    kernel_hbm = pltpu.with_memory_space_constraint(kernel, pltpu.HBM)
    for c, place in enumerate([places_of(groups) for groups in chunks]):
        own_part, *parts, rows = cotangent_part(meta, w[c], chunks[c], kernel_hbm, place, depth, (pltpu.HBM, pltpu.VMEM)[c])
        cots.append(spread(own_part, parts))
        whole.append(rows)
    scale = float(1.0 / (float(pixels) ** 0.5))
    product = product_of(
        meta,
        [(whole[c], *xts[c]) for c in range(2)],
        [len(groups) for groups in chunks],
        scale,
        channels,
        own,
    )
    result = jnp.where(
        lax.rem(z, 2) == 0, jnp.concatenate(cots, axis=0), jnp.concatenate(cots[::-1], axis=0)
    )
    return (result, product)


def block_device(*args):
    return block_program(*args)


def fits(mesh, pixels, channels, filters):
    depth, across = mesh.shape["filt"], mesh.shape["chan"]
    images = pixels // (HH * WW)
    return (
        depth == 2 * PAIR
        and 2 * images == 9 * depth
        and across == 8
        and 2 * channels == LANES * across * depth
        and filters == LANES * (across // 2) * depth
    )


def solution(mesh):
    in_specs = (
        P(None, ("chan", "filt")),
        P(None, ("chan", "filt")),
        P(None, "chan", "filt"),
        P(None, "chan", "filt"),
        P("chan", "filt"),
        P("chan", "filt"),
    )

    def program(*args):
        pixels, channels = args[0].shape
        body = block_device if fits(mesh, pixels, channels, args[2].shape[2]) else any_device
        return jax.shard_map(
            body,
            mesh=mesh,
            in_specs=in_specs,
            out_specs=(P("filt", "chan"), P(None, "chan", "filt")),
            check_vma=False,
        )(*args)

    return program
```

```python
import functools

import jax
import jax.numpy as jnp
from jax import lax
from jax.experimental import pallas as pl
from jax.experimental.pallas import tpu as pltpu
from jax.sharding import PartitionSpec as P


HH = 12
WW = 12
LANES = 128
STRIPS = 4
DEEP = HH // STRIPS
PAIR = 2
EIGHT = PAIR * STRIPS
PIECE = WW * EIGHT
GROUP = DEEP * PIECE
SPARE = 64

INNER = 1
PARAMS = pltpu.CompilerParams(vmem_limit_bytes=28 << 20)


def windows(flat, flip):
    width = flat.shape[-1]
    image = flat.reshape(-1, HH, WW, width)
    padded = jnp.pad(image, ((0, 0), (1, 1), (1, 1), (0, 0)))
    result = []
    for row_tap in range(3):
        for col_tap in range(3):
            top = 2 - row_tap if flip else row_tap
            left = 2 - col_tap if flip else col_tap
            result.append(padded[:, top : top + HH, left : left + WW, :].reshape(-1, width))
    return result


def weigh(slope, curvature, tangent):
    slope_f = slope.astype(jnp.float32)
    return (slope_f * slope_f * curvature.astype(jnp.float32) * tangent).astype(jnp.bfloat16)


def any_device(activations, act_tangent, kernel, kernel_tangent, slope, curvature):
    acts_block, tans_block = (
        lax.all_gather(activations, "filt", axis=1, tiled=True),
        lax.all_gather(act_tangent, "filt", axis=1, tiled=True),
    )
    acts = windows(acts_block, False)
    tans = windows(tans_block, False)
    pixel_count = acts_block.shape[0]
    partial_value = jnp.zeros((pixel_count, kernel.shape[2]), jnp.float32)
    for tap in range(9):
        partial_value = partial_value + jnp.dot(
            tans[tap], kernel[tap], preferred_element_type=jnp.float32
        )
        partial_value = partial_value + jnp.dot(
            acts[tap], kernel_tangent[tap], preferred_element_type=jnp.float32
        )
    total = lax.psum(partial_value, "chan")
    slope_all, curve_all = (
        lax.all_gather(slope, "chan", axis=0, tiled=True),
        lax.all_gather(curvature, "chan", axis=0, tiled=True),
    )
    weighted = weigh(slope_all, curve_all, total)
    backs = windows(weighted, True)
    cot_part = jnp.zeros((pixel_count, kernel.shape[1]), jnp.float32)
    grads = []
    for tap in range(9):
        cot_part = cot_part + lax.dot_general(
            backs[tap], kernel[tap], (((1,), (1,)), ((), ())), preferred_element_type=jnp.float32
        )
        grads.append(
            lax.dot_general(
                acts[tap], weighted, (((0,), (0,)), ((), ())), preferred_element_type=jnp.float32
            )
        )
    kernel_product = jnp.stack(grads) / jnp.sqrt(jnp.float32(pixel_count))
    cotangent = lax.psum_scatter(cot_part, "filt", scatter_dimension=0, tiled=True).astype(
        jnp.bfloat16
    )
    return (cotangent, kernel_product)


def pieces_of(groups):
    for g, images in enumerate(groups):
        for strip in range(EIGHT):
            image, part = images[strip // STRIPS], strip % STRIPS
            for deep in range(DEEP):
                source = (image * HH + part * DEEP + deep) * WW
                yield g, strip, deep, source, (deep * len(groups) + g) * PIECE + strip


def sort_into(chunks, flat, sorted_, outs, cols):
    for groups, out in zip(chunks, outs):
        for _, _, _, source, target in pieces_of(groups):
            sorted_[pl.ds(target, WW, stride=EIGHT), :] = flat[pl.ds(source, WW), :]
        out[:, cols] = sorted_[pl.ds(0, out.shape[0]), :].astype(out.dtype)


def sort_kernel(chunks, x_ref, *refs):
    outs, (flat, sorted_) = refs[: len(chunks)], refs[len(chunks) :]
    blocks, each = x_ref.shape[0], x_ref.shape[1] // 2
    rows = (flat.shape[0] - SPARE) // blocks
    for kind in range(2):
        for n in range(blocks):
            block = x_ref[n, kind * each : (kind + 1) * each, :].astype(jnp.float32)
            flat[n * rows : (n + 1) * rows, :] = block[:rows]
        sort_into(chunks, flat, sorted_, outs, pl.ds(kind * LANES, LANES))


def mix_kernel(chunks, a_ref, t_ref, *refs):
    outs, (flat, sorted_) = refs[: len(chunks)], refs[len(chunks) :]
    both = jnp.concatenate(
        [a_ref[...].astype(jnp.float32), t_ref[...].astype(jnp.float32)], axis=0
    )
    flat[pl.ds(0, both.shape[1]), :] = both.T
    sort_into(chunks, flat, sorted_, outs, pl.ds(0, LANES))


def sort_call(kernel, chunks, given, pixels, width):
    rows = [len(groups) * GROUP for groups in chunks]
    return pl.pallas_call(
        functools.partial(kernel, chunks),
        out_shape=[jax.ShapeDtypeStruct((r, width), given[0].dtype) for r in rows],
        scratch_shapes=[
            pltpu.VMEM((pixels + SPARE, LANES), jnp.float32),
            pltpu.VMEM((max(rows) + SPARE, LANES), jnp.float32),
        ],
        compiler_params=PARAMS,
    )(*given)


def copy_all(copies):
    for copy in copies:
        copy.start()
    for copy in copies:
        copy.wait()


def build(x_ref, views, groups):
    width = x_ref.shape[1]
    strip = lax.broadcasted_iota(jnp.int32, (PIECE, width), 0) % STRIPS

    def put(at, block):
        at = pl.multiple_of(at, PIECE)
        none = jnp.zeros((EIGHT, width), jnp.float32)
        views[1, pl.ds(at, PIECE), :] = block.astype(jnp.bfloat16)
        before = jnp.concatenate([none, block[: PIECE - EIGHT]], axis=0)
        views[0, pl.ds(at, PIECE), :] = before.astype(jnp.bfloat16)
        after = jnp.concatenate([block[EIGHT:], none], axis=0)
        views[2, pl.ds(at, PIECE), :] = after.astype(jnp.bfloat16)

    def load(at):
        return x_ref[pl.ds(pl.multiple_of(at, PIECE), PIECE), :].astype(jnp.float32)

    def turn(block, by):
        return pltpu.roll(block.reshape(WW, EIGHT, width), by, 1).reshape(PIECE, width)

    @pl.loop(0, DEEP * groups)
    def _(n):
        put((groups + n) * PIECE, load(n * PIECE))

    @pl.loop(0, groups)
    def _(g):
        above = turn(load(((DEEP - 1) * groups + g) * PIECE), 1)
        put(g * PIECE, jnp.where(strip == 0, 0.0, above))
        below = turn(load(g * PIECE), EIGHT - 1)
        put(((DEEP + 1) * groups + g) * PIECE, jnp.where(strip == STRIPS - 1, 0.0, below))


def tap_rows(views, groups, row, col):
    start = row * (groups * PIECE)
    if not isinstance(row, int):
        start = pl.multiple_of(start, PIECE)
    return views[col, pl.ds(start, groups * GROUP), :]


def views_shape(groups, width):
    return pltpu.VMEM((3, (DEEP + 2) * groups * PIECE, width), jnp.bfloat16)


HALF, CHIP, PLACE, SHARDS = 0, 1, 2, 3


def tangent_kernel(groups, sources, slots, more, last, meta, *refs):
    count = len(slots)
    given = 1 + max(n for order in sources for n in order)
    shards = refs[:given]
    v_ref, w_ref = refs[given : given + 2]
    before = refs[given + 2] if more else None
    refs = refs[given + 2 + more :]
    if last:
        send_ref, keep_ref, xt_ref, x, xt, views, sem, *refs = refs
        acc, *refs = refs
    else:
        acc, xt_ref, x, xt, views, sem, *refs = refs
    away = pltpu.make_async_copy(xt, xt_ref, sem.at[count + 2])
    own = v_ref.shape[1] // len(sources)
    step = pl.program_id(0)

    @pl.when(step == 0)
    def _():
        fetch = []
        if count == 1:
            at = pl.ds(pl.multiple_of(meta[SHARDS + slots[0]] * own, own), own)
            for n, ref in enumerate((v_ref, w_ref)):
                to = refs[0].at[:, pl.ds(n * own, own), :]
                fetch.append(pltpu.make_async_copy(ref.at[:, at, :], to, sem.at[count + n]))
        for copy in fetch:
            copy.start()
        for z, order in enumerate(sources):

            @pl.when(meta[PLACE] == z)
            def _():
                copy_all(
                    [
                        pltpu.make_async_copy(
                            shards[n],
                            x.at[:, pl.ds(i * LANES, LANES)],
                            sem.at[i],
                        )
                        for i, n in enumerate(order)
                    ]
                )

        build(x, views, groups)
        for i in range(count):
            turned = x[:, i * LANES : (i + 1) * LANES].astype(jnp.float32).T
            xt[i * own : (i + 1) * own, :] = turned[:own].astype(jnp.bfloat16)
        away.start()
        for copy in fetch:
            copy.wait()

    if count == 1:
        lhs = [tap_rows(views, groups, row, col) for row in range(3) for col in range(3)]
        rhs = refs[0][...].reshape(9 * LANES, acc.shape[1])
    else:
        lhs, rhs = [], []
        for col in range(3):
            lhs.append(tap_rows(views, groups, step, col))
            for slot in slots:
                at = pl.ds(pl.multiple_of(meta[SHARDS + slot] * own, own), own)
                rhs += [v_ref[col, at, :], w_ref[col, at, :]]
        rhs = jnp.concatenate(rhs, axis=0)
    value = jnp.dot(jnp.concatenate(lhs, axis=1), rhs, preferred_element_type=jnp.float32)
    pl.when(step == pl.num_programs(0) - 1)(away.wait)
    if count == 1:
        acc[...] = before[...] + value if more else value
    elif more:
        acc[...] = value + jnp.where(step == 0, before[...], acc[...])
    else:
        acc[...] = jnp.where(step == 0, value, acc[...] + value)
    if last:
        pl.when(step == pl.num_programs(0) - 1)(
            functools.partial(halves, meta, acc, send_ref, keep_ref)
        )


def halves(meta, acc, send_ref, keep_ref):
    half, n = meta[HALF], acc.shape[0] // 2
    mine = pl.ds(pl.multiple_of(half * n, n), n)
    other = pl.ds(pl.multiple_of((1 - half) * n, n), n)
    send_ref[...] = acc[other, :].astype(jnp.bfloat16)
    keep_ref[...] = acc[mine, :]


def tangent(meta, shards, sources, slots, v, w, groups, before, last):
    more = before is not None
    rows = groups * GROUP
    channels, filters = w.shape[1:]
    count = len(slots)
    own = channels // len(sources)
    whole_block = pl.BlockSpec(memory_space=pl.ANY)
    row_block = pl.BlockSpec((3, channels, filters), lambda t, m: (t, 0, 0))

    def whole(*shape):
        return pl.BlockSpec(shape, lambda t, m: (0,) * len(shape))

    hbm = pl.BlockSpec(memory_space=pltpu.HBM)
    if last:
        out_specs = [whole(rows // 2, filters)] * 2
        outs = [
            jax.ShapeDtypeStruct((rows // 2, filters), jnp.bfloat16),
            jax.ShapeDtypeStruct((rows // 2, filters), jnp.float32),
        ]
    else:
        out_specs = [whole(rows, filters)]
        outs = [jax.ShapeDtypeStruct((rows, filters), jnp.float32)]
    return pl.pallas_call(
        functools.partial(tangent_kernel, groups, sources, slots, more, last),
        grid_spec=pltpu.PrefetchScalarGridSpec(
            num_scalar_prefetch=1,
            grid=(1 if count == 1 else 3,),
            in_specs=[whole_block] * len(shards)
            + [whole_block if count == 1 else row_block] * 2
            + ([whole(rows, filters)] if more else []),
            out_specs=out_specs + [hbm],
            scratch_shapes=[
                pltpu.VMEM((rows, count * LANES), jnp.bfloat16),
                pltpu.VMEM((count * own, rows), jnp.bfloat16),
                views_shape(groups, count * LANES),
                pltpu.SemaphoreType.DMA((count + 3,)),
            ]
            + ([pltpu.VMEM((rows, filters), jnp.float32)] if last else [])
            + ([pltpu.VMEM((9, LANES, filters), jnp.bfloat16)] if count == 1 else []),
        ),
        out_shape=outs + [pltpu.HBM((count * own, rows), jnp.bfloat16)],
        cost_estimate=pl.CostEstimate(
            flops=18 * rows * count * LANES * filters,
            bytes_accessed=4 * w.size,
            transcendentals=0,
        ),
        name="tangent",
        compiler_params=PARAMS,
    )(meta, *shards, v, w, *([before] if more else []))


def split_kernel(meta, keep_ref, got_ref, mine_ref, *parts):
    for m in range(1 + len(parts)):
        at = pl.multiple_of((meta[CHIP] ^ m) * LANES, LANES)
        total = keep_ref[:, pl.ds(at, LANES)] + got_ref[:, pl.ds(at, LANES)].astype(jnp.float32)
        if m:
            parts[m - 1][...] = total.astype(jnp.bfloat16)
        else:
            mine_ref[...] = total


def split(meta, keep, got):
    rows, filters = keep.shape
    block = pl.BlockSpec((rows, filters), lambda t, m: (0, 0))
    out = pl.BlockSpec((rows, LANES), lambda t, m: (0, 0))
    kinds = [jnp.float32] + [jnp.bfloat16] * (filters // LANES - 1)
    return pl.pallas_call(
        split_kernel,
        grid_spec=pltpu.PrefetchScalarGridSpec(
            num_scalar_prefetch=1, grid=(1,), in_specs=[block] * 2, out_specs=[out] * len(kinds)
        ),
        out_shape=[jax.ShapeDtypeStruct((rows, LANES), kind) for kind in kinds],
        cost_estimate=pl.CostEstimate(
            flops=rows * filters, bytes_accessed=8 * keep.size, transcendentals=0
        ),
        name="split",
        compiler_params=PARAMS,
    )(meta, keep, got)


def gather_parts(meta, parts, x, sem):
    blocks, rows = len(parts) // 2, x.shape[0] // 2
    copies = []
    for n, part in enumerate(parts):
        half = meta[HALF] if n < blocks else 1 - meta[HALF]
        at = pl.multiple_of(half * rows, rows)
        lane = pl.multiple_of((meta[CHIP] ^ (n % blocks)) * LANES, LANES)
        to = x.at[pl.ds(at, rows), pl.ds(lane, LANES)]
        copies.append(pltpu.make_async_copy(part, to, sem.at[n]))
    copy_all(copies)


def cotangent_kernel(groups, places, parts, meta, *refs):
    outs = refs[-6 - parts : -6]
    w_parts, k_ref = refs[: -7 - parts], refs[-7 - parts]
    rows_ref, x, views, sem, acc, flat = refs[-6:]
    step = pl.program_id(0)
    keep = pltpu.make_async_copy(x, rows_ref, sem.at[len(w_parts)])

    @pl.when(step == 0)
    def _():
        gather_parts(meta, w_parts, x, sem)
        keep.start()
        build(x, views, len(groups))

    value = lax.dot_general(
        jnp.concatenate(
            [tap_rows(views, len(groups), 2 - step, 2 - col) for col in range(3)], axis=1
        ),
        jnp.concatenate([k_ref[col] for col in range(3)], axis=1),
        (((1,), (1,)), ((), ())),
        preferred_element_type=jnp.float32,
    )
    for n in range(acc.shape[0]):
        column = value[:, n * LANES : (n + 1) * LANES]
        acc[n, : x.shape[0]] = jnp.where(step == 0, column, acc[n, : x.shape[0]] + column)

    @pl.when(step == 2)
    def _():
        keep.wait()
        for n in range(acc.shape[0]):
            for g, strip, deep, _, row in pieces_of(groups):
                target = places[g, strip] + deep * WW
                flat[pl.ds(target, WW), :] = acc[n, pl.ds(row, WW, stride=EIGHT), :]
            share = x.shape[0] // parts
            for m, out in enumerate(outs):
                at = pl.multiple_of((meta[PLACE] ^ m) * share, share)
                cols = pl.ds(n * LANES, LANES)
                out[:, cols] = flat[pl.ds(at, share), :].astype(out.dtype)


def cotangent_part(meta, w_parts, groups, kernel, places, parts, rows_space):
    channels, filters = kernel.shape[1:]
    rows = 2 * w_parts[0].shape[0]
    return pl.pallas_call(
        functools.partial(cotangent_kernel, groups, places, parts),
        grid_spec=pltpu.PrefetchScalarGridSpec(
            num_scalar_prefetch=1,
            grid=(3,),
            in_specs=[pl.BlockSpec(memory_space=pl.ANY)] * len(w_parts)
            + [pl.BlockSpec((3, channels, filters), lambda t, m: (t, 0, 0))],
            out_specs=[pl.BlockSpec((rows // parts, channels), lambda t, m: (0, 0))] * parts
            + [pl.BlockSpec(memory_space=rows_space)],
            scratch_shapes=[
                pltpu.VMEM((rows, filters), jnp.bfloat16),
                views_shape(len(groups), filters),
                pltpu.SemaphoreType.DMA((len(w_parts) + 1,)),
                pltpu.VMEM((channels // LANES, rows + SPARE, LANES), jnp.float32),
                pltpu.VMEM((rows + SPARE, LANES), jnp.float32),
            ],
        ),
        out_shape=[
            jax.ShapeDtypeStruct((rows // parts, channels), jnp.bfloat16 if m else jnp.float32)
            for m in range(parts)
        ]
        + [rows_space((rows, filters), jnp.bfloat16)],
        cost_estimate=pl.CostEstimate(
            flops=18 * rows * channels * filters,
            bytes_accessed=18 * channels * filters,
            transcendentals=0,
        ),
        name="cotangent",
        compiler_params=PARAMS,
    )(meta, *w_parts, kernel)


def product_kernel(own, counts, sizes, scale, meta, *refs):
    chunks = len(counts)
    scratch = refs[-2 * chunks :]
    given, out_ref = refs[: -1 - 2 * chunks], refs[-1 - 2 * chunks]
    ends = [sum(sizes[: n + 1]) for n in range(chunks)]
    tap = pl.program_id(0)

    @pl.when(tap == 0)
    def _():
        for n, count in enumerate(counts):
            w_ref, *xts = given[ends[n] - sizes[n] : ends[n]]
            views, xt = scratch[2 * n : 2 * n + 2]
            build(w_ref, views, count)
            slot = 0
            for ref in xts:
                for row in range(0, ref.shape[0], own):
                    at = pl.multiple_of(meta[SHARDS + slot] * own, own)
                    xt[pl.ds(at, own), :] = ref[pl.ds(row, own), :]
                    slot += 1

    value = None
    for n, count in enumerate(counts):
        views, xt = scratch[2 * n : 2 * n + 2]
        term = jnp.dot(
            xt[...], tap_rows(views, count, 2 - tap // 3, 2 - lax.rem(tap, 3)), preferred_element_type=jnp.float32
        )
        value = term if value is None else value + term
    out_ref[0] = value * scale


def product_of(meta, chunks, counts, scale, channels, own):
    given = [array for chunk in chunks for array in chunk]
    total = sum(chunk[0].shape[0] for chunk in chunks)
    filters = chunks[0][0].shape[1]
    scratch = []
    for (w, *_), count in zip(chunks, counts):
        scratch += [views_shape(count, filters), pltpu.VMEM((channels, w.shape[0]), jnp.bfloat16)]
    return pl.pallas_call(
        functools.partial(product_kernel, own, counts, [len(chunk) for chunk in chunks], scale),
        grid_spec=pltpu.PrefetchScalarGridSpec(
            num_scalar_prefetch=1,
            grid=(9,),
            in_specs=[pl.BlockSpec(array.shape, lambda t, m: (0, 0)) for array in given],
            out_specs=pl.BlockSpec((1, channels, filters), lambda t, m: (t, 0, 0)),
            scratch_shapes=scratch,
        ),
        out_shape=jax.ShapeDtypeStruct((9, channels, filters), jnp.float32),
        cost_estimate=pl.CostEstimate(
            flops=18 * total * channels * filters,
            bytes_accessed=36 * channels * filters,
            transcendentals=0,
        ),
        name="product",
        compiler_params=PARAMS,
    )(meta, *given)


def pack_kernel(s_ref, c_ref, out_ref):
    rows = s_ref.shape[0]
    each = out_ref.shape[1] // 2
    for n in range(out_ref.shape[0]):
        cols = pl.ds(n // 2 * LANES, LANES)
        for kind, ref in enumerate((s_ref, c_ref)):
            out_ref[n, kind * each : kind * each + rows, :] = ref[:, cols]
            rest = jnp.zeros((each - rows, LANES), out_ref.dtype)
            out_ref[n, kind * each + rows : (kind + 1) * each, :] = rest


def pack(slope, curvature):
    rows, filters = slope.shape
    each = -(-rows // 16) * 16
    return pl.pallas_call(
        pack_kernel,
        out_shape=jax.ShapeDtypeStruct((2 * filters // LANES, 2 * each, LANES), slope.dtype),
        name="pack",
        compiler_params=PARAMS,
    )(slope, curvature)


def block_program(activations, act_tangent, kernel, kernel_tangent, slope, curvature):
    z, me = lax.axis_index("filt"), lax.axis_index("chan")
    depth, across = lax.axis_size("filt"), lax.axis_size("chan")
    half, chips = lax.rem(me, 2), across // 2
    pixels, own = activations.shape
    channels = kernel.shape[1]

    per = 2 * (pixels // (HH * WW)) // depth
    outer, inner = [], []
    for image in range(per * depth // 2):
        (inner if abs(image % per - per // 2) <= INNER else outer).append(image)
    chunks = [list(zip(images[::PAIR], images[1::PAIR])) for images in (outer, inner)]

    orders, owners = [], []
    for place in range(depth):
        order, owner = [(0, 0)], [place]
        for step in range(1, depth):
            for link in range(2):
                shard = place + step if place % 2 == link else place - step
                if 0 <= shard < depth:
                    order.append((step, link))
                    owner.append(shard)
        orders.append(order)
        owners.append(owner)
    table = [
        [n % 2, n // 2, place] + owners[place]
        for place in range(depth)
        for n in range(across)
    ]
    meta = lax.dynamic_index_in_dim(
        jnp.asarray(table, jnp.int32), z * across + me, 0, keepdims=False
    )

    mixed = sort_call(
        mix_kernel,
        chunks,
        [pltpu.with_memory_space_constraint(x.T, pltpu.HBM) for x in (activations, act_tangent)],
        pixels,
        2 * own,
    )

    packed = pack(slope, curvature)
    packed = lax.all_to_all(packed, "chan", 0, 0, tiled=True)
    factors = sort_call(sort_kernel, chunks, [packed], pixels, 2 * LANES)

    def gathered(x):
        got = {(0, 0): x}
        last = [x, x]
        for step in range(1, depth):
            now = [None, None]
            for link in range(2):
                pairs = []
                for i in range(link, depth - 1, 2):
                    pairs += [(i, i + 1)] * (i >= step - 1) + [(i + 1, i)] * (i + 1 <= depth - step)
                if pairs:
                    now[link] = lax.ppermute(last[1 - link], "filt", pairs)
                    got[step, link] = now[link]
            last = now
        return got

    def swap(x, bit):
        return lax.ppermute(x, "chan", [(i, i ^ bit) for i in range(across)])

    def some(slots, c):
        names = sorted({order[slot] for order in orders for slot in slots})
        sources = [[names.index(order[slot]) for slot in slots] for order in orders]
        return [got[c][name] for name in names], sources

    def tangents(c):
        stages = [[0, 1], [2], [3]] if c == 0 else [[0, 1], [2, 3]]
        before, xts = None, []
        for n, slots in enumerate(stages):
            shards, sources = some(slots, c)
            *sums, xt = tangent(
                meta,
                shards,
                sources,
                slots,
                pltpu.with_memory_space_constraint(kernel_tangent, pltpu.HBM),
                pltpu.with_memory_space_constraint(kernel, pltpu.HBM),
                len(chunks[c]),
                before,
                n == len(stages) - 1,
            )
            before = sums[0]
            xts.append(xt)
        return sums, xts

    def exchange(send, keep):
        got = swap(send, 1)
        mine, *parts = split(meta, keep, got)
        for m, part in enumerate(parts):
            mine = mine + swap(part, 2 * (m + 1)).astype(jnp.float32)
        return mine

    def weighted(mine, factor, c):
        rows = mine.shape[0]
        factor = lax.dynamic_slice_in_dim(factor, half * rows, rows, axis=0)
        w = weigh(factor[:, :LANES], factor[:, LANES:], mine)
        parts = [w] + [swap(w, 2 * m) for m in range(1, chips)]
        parts += [swap(part, 1) for part in parts]
        if c == 0:
            parts = [pltpu.with_memory_space_constraint(part, pltpu.HBM) for part in parts]
        return parts

    def places_of(groups):
        strip_rows = GROUP // EIGHT
        sources = {}
        for g, images in enumerate(groups):
            for strip in range(EIGHT):
                row = images[strip // STRIPS] * HH * WW + strip % STRIPS * strip_rows
                sources[row] = (g, strip)
        return {sources[row]: n * strip_rows for n, row in enumerate(sorted(sources))}

    def spread(own_part, parts):
        total = own_part
        for m, part in enumerate(parts):
            part = lax.ppermute(part, "filt", [(i, i ^ (m + 1)) for i in range(depth)])
            total = total + part.astype(jnp.float32)
        return total.astype(jnp.bfloat16)

    got = [gathered(x) for x in mixed]
    sums, xts = zip(*[tangents(c) for c in range(2)])
    mine = [exchange(*sums[c]) for c in range(2)]
    w = [weighted(mine[c], factors[c], c) for c in range(2)]
    cots, whole = [], []
    kernel_hbm = pltpu.with_memory_space_constraint(kernel, pltpu.HBM)
    for c, place in enumerate([places_of(groups) for groups in chunks]):
        own_part, *parts, rows = cotangent_part(meta, w[c], chunks[c], kernel_hbm, place, depth, (pltpu.HBM, pltpu.VMEM)[c])
        cots.append(spread(own_part, parts))
        whole.append(rows)
    scale = float(1.0 / (float(pixels) ** 0.5))
    product = product_of(
        meta,
        [(whole[c], *xts[c]) for c in range(2)],
        [len(groups) for groups in chunks],
        scale,
        channels,
        own,
    )
    result = jnp.where(
        lax.rem(z, 2) == 0, jnp.concatenate(cots, axis=0), jnp.concatenate(cots[::-1], axis=0)
    )
    return (result, product)


def block_device(*args):
    return block_program(*args)


def fits(mesh, pixels, channels, filters):
    depth, across = mesh.shape["filt"], mesh.shape["chan"]
    images = pixels // (HH * WW)
    return (
        depth == 2 * PAIR
        and 2 * images == 9 * depth
        and across == 8
        and 2 * channels == LANES * across * depth
        and filters == LANES * (across // 2) * depth
    )


def solution(mesh):
    in_specs = (
        P(None, ("chan", "filt")),
        P(None, ("chan", "filt")),
        P(None, "chan", "filt"),
        P(None, "chan", "filt"),
        P("chan", "filt"),
        P("chan", "filt"),
    )

    def program(*args):
        pixels, channels = args[0].shape
        body = block_device if fits(mesh, pixels, channels, args[2].shape[2]) else any_device
        return jax.shard_map(
            body,
            mesh=mesh,
            in_specs=in_specs,
            out_specs=(P("filt", "chan"), P(None, "chan", "filt")),
            check_vma=False,
        )(*args)

    return program
```
